512 devices in a mesh: ctx: 64 (over x, y, core), head: 8 (over z).
Axes of the slice: x: 4, y: 8, z: 8, core: 2. Of those that a mesh axis runs over, the one named last changes fastest.
Arguments:
- placement: int32 [64], replicated, may hold values from 0 to 63, each once
- placed_queries: bfloat16 [16384, 4096], P('ctx', 'head'), may hold values from -160 to 160
- placed_keys: bfloat16 [16384, 1024], P('ctx', 'head'), may hold values from -4.5 to 4.5
- placed_values: bfloat16 [16384, 1024], P('ctx', 'head'), may hold values from -6 to 6
- out_weight: bfloat16 [4096, 4096], P('head', 'ctx'), may hold values from -0.25 to 0.25
Outputs:
- attention_out: bfloat16 [16384, 4096], P('ctx', 'head')
The draws below stay inside these ranges and needn't reach their ends.
Inputs may be any that keep to these rules, and one draw needn't show every extreme that they name: placement holds each of 0 .. 63 once.
All inputs are finite; a program needn't handle non-finite values.
Results may differ from the reference program's by a relative error of at most 0.015.
Values may be sent and summed in bfloat16 or wider, within the bound.
No kernel may reach another device: no remote copies, remote signals or barrier semaphores. Data moves between devices by JAX's collectives and lax.ppermute only.
A program may use at most 64 MiB of HBM per device.

```python
import jax
import jax.numpy as jnp
from jax import lax

D = 4096
QUERY_HEADS = 32
KEY_VALUE_HEADS = 8
HEAD_FEATURES = 128
TOKENS_PER_PART = 256
SEQUENCE_TOKENS = 16384
N_CTX = 64
N_HEAD = 8


def shared_keys(key):
    random_seed_key = jax.random.fold_in(key, 11)
    sampled = jnp.clip(jax.random.normal(random_seed_key, (SEQUENCE_TOKENS, KEY_VALUE_HEADS * HEAD_FEATURES), jnp.float32), -4.5, 4.5)
    return sampled


def draw_placed_keys(key, part):
    return shared_keys(key).astype(jnp.bfloat16)


def draw_placed_queries(key, part):
    sampled = jnp.clip(jax.random.normal(jax.random.fold_in(key, 13), (SEQUENCE_TOKENS, QUERY_HEADS * HEAD_FEATURES), jnp.float32), -4.5, 4.5)
    return sampled.astype(jnp.bfloat16)


def with_spikes(values, stream_key, source, target, parts, factor):
    def block_of(dim):
        return (jnp.arange(values.shape[dim]) // (values.shape[dim] // parts)).reshape((-1,) + (1,) * (values.ndim - 1 - dim))

    near = jax.random.permutation(stream_key, parts)[block_of(target)]
    other_side = (block_of(target) + parts // 2) % parts
    return jnp.where((block_of(source) == near) | (block_of(source) == other_side), factor * values, values)


def block_levels(rng, shape, cuts, low, top_value):
    factor_of, own = 1.0, jax.random.fold_in(rng, 6)
    for axis_at, shards_of in cuts:
        steps = jnp.exp(jax.random.uniform(jax.random.fold_in(own, axis_at), (shards_of,), jnp.float32, low / len(cuts), top_value / len(cuts)))
        factor_of = factor_of * jnp.repeat(steps, shape[axis_at] // shards_of).reshape([-1 if axis == axis_at else 1 for axis in range(len(shape))])
    return factor_of


def centred(rng, shape, scale, reach, cuts=(), held_as=jnp.bfloat16):
    values = scale * jax.random.normal(rng, shape, jnp.float32)
    if cuts:
        values = values * block_levels(rng, shape, cuts, -0.22, 0.18)
    return jnp.clip(values, -reach, reach).astype(held_as)


def gaussian_with(key, shape, deviation, limit, cuts, heavy, kind=jnp.bfloat16):
    drawn = deviation * jax.random.normal(key, shape, jnp.float32)
    if cuts:
        drawn = drawn * block_levels(key, shape, cuts, -0.22, 0.18)
    return jnp.clip(with_spikes(drawn, jax.random.fold_in(key, 3), *heavy), -limit, limit).astype(kind)


def setup_inputs(seed: int = 0) -> dict:
    keys = jax.random.split(jax.random.key(seed), 6)
    placement = jax.random.permutation(keys[0], N_CTX).astype(jnp.int32)
    placed_queries = draw_placed_queries(jax.random.fold_in(keys[5], 71), 0)
    placed_keys = draw_placed_keys(jax.random.fold_in(keys[5], 71), 0)
    placed_values = centred(keys[3], (SEQUENCE_TOKENS, KEY_VALUE_HEADS * HEAD_FEATURES), 1.0, 6.0, ((0, 64), (1, 8)))
    out_weight = gaussian_with(keys[4], (QUERY_HEADS * HEAD_FEATURES, D), (QUERY_HEADS * HEAD_FEATURES) ** -0.5, 0.25, ((0, 8), (1, 64)), (0, 1, 64, 4.0))
    return {"placement": placement, "placed_queries": placed_queries, "placed_keys": placed_keys, "placed_values": placed_values, "out_weight": out_weight}


masked_score = -1.0e30


def causal_softmax(placement, placed_queries, placed_keys, placed_values):
    order_indices = jnp.argsort(placement)
    model_width = QUERY_HEADS * HEAD_FEATURES
    common_across = QUERY_HEADS // KEY_VALUE_HEADS
    sequence_queries = placed_queries.reshape(N_CTX, TOKENS_PER_PART, model_width)[order_indices].reshape(SEQUENCE_TOKENS, KEY_VALUE_HEADS, common_across, HEAD_FEATURES)
    sequence_keys = placed_keys.reshape(N_CTX, TOKENS_PER_PART, KEY_VALUE_HEADS * HEAD_FEATURES)[order_indices].reshape(SEQUENCE_TOKENS, KEY_VALUE_HEADS, HEAD_FEATURES)
    sequence_values = placed_values.reshape(N_CTX, TOKENS_PER_PART, KEY_VALUE_HEADS * HEAD_FEATURES)[order_indices].reshape(SEQUENCE_TOKENS, KEY_VALUE_HEADS, HEAD_FEATURES)
    block_rows = SEQUENCE_TOKENS // 16
    results = []
    for member in range(16):
        low_row = member * block_rows
        high_row = low_row + block_rows
        query_block = jnp.transpose(sequence_queries[low_row:high_row], (1, 2, 0, 3)).astype(jnp.float32)
        key_block = jnp.transpose(sequence_keys[:high_row], (1, 0, 2)).astype(jnp.float32)
        value_block = jnp.transpose(sequence_values[:high_row], (1, 0, 2)).astype(jnp.float32)
        query_pos = low_row + jnp.arange(block_rows, dtype=jnp.int32)
        key_pos = jnp.arange(high_row, dtype=jnp.int32)
        allowed = key_pos[None, :] <= query_pos[:, None]

        def one_head(operands):
            head_queries, head_keys, head_values = operands
            scores = jnp.einsum("grd,sd->grs", head_queries, head_keys) * (HEAD_FEATURES ** -0.5)
            scores = jnp.where(allowed, scores, masked_score)
            peak = jnp.max(scores, axis=-1, keepdims=True)
            weights = jnp.where(allowed, jnp.exp(scores - peak), 0.0)
            norm_sum = jnp.sum(weights, axis=-1)
            rounded = lax.optimization_barrier(weights.astype(jnp.bfloat16)).astype(jnp.float32)
            return jnp.einsum("grs,sd->grd", rounded, head_values) / norm_sum[..., None]

        block_out = lax.map(one_head, (query_block, key_block, value_block))
        results.append(jnp.transpose(block_out, (2, 0, 1, 3)).reshape(block_rows, model_width).astype(jnp.bfloat16))
    seq_out = jnp.concatenate(results, axis=0)
    return seq_out.reshape(N_CTX, TOKENS_PER_PART, model_width)[placement].reshape(SEQUENCE_TOKENS, model_width)


def reference(placement, placed_queries, placed_keys, placed_values, out_weight):
    hidden = causal_softmax(placement, placed_queries, placed_keys, placed_values)
    width_dev = QUERY_HEADS * HEAD_FEATURES // N_HEAD
    summed = jnp.zeros((SEQUENCE_TOKENS, D), jnp.float32)
    for member in range(N_HEAD):
        term = jnp.dot(hidden[:, member * width_dev:(member + 1) * width_dev], out_weight[member * width_dev:(member + 1) * width_dev], preferred_element_type=jnp.float32)
        summed = summed + lax.optimization_barrier(term.astype(jnp.bfloat16)).astype(jnp.float32)
    return summed.astype(jnp.bfloat16)
```

```python
import functools

import jax
import jax.numpy as jnp
from jax import lax
from jax.experimental import pallas as pl
from jax.experimental.pallas import tpu as pltpu
from jax.sharding import PartitionSpec as P

HEAD_FEATURES = 128
CHUNK_BLOCKS = 4
MASKED = -1e30
LOG2_E = 1.4426950408889634


def attend_kernel(blocks, rows, heads, groups, place_ref, q_ref, all_ref, out_ref,
                  order, kv, wt, top, total, acc, hidden, kv_sem, wt_sem):
    features = HEAD_FEATURES
    width = 2 * features
    weight_rows = wt.shape[1]
    factor = features ** (-0.5) * LOG2_E
    own = place_ref[lax.axis_index("ctx")]
    last_chunk = own // CHUNK_BLOCKS
    held = (last_chunk + 1) * CHUNK_BLOCKS

    @pl.loop(0, blocks)
    def _(j):
        order[place_ref[j]] = j

    def fetch(p):
        return pltpu.make_async_copy(
            all_ref.at[order[p], pl.ds(0, rows), :], kv.at[p], kv_sem.at[p]
        )

    @pl.loop(0, held)
    def _(p):
        fetch(p).start()

    weight_copy = pltpu.make_async_copy(
        all_ref.at[:, pl.ds(rows, weight_rows), :], wt, wt_sem
    )
    weight_copy.start()

    top[...] = jnp.full_like(top, MASKED)
    total[...] = jnp.zeros_like(total)
    acc[...] = jnp.zeros_like(acc)
    chunk_rows = CHUNK_BLOCKS * rows

    def step(chunk, masked):
        for i in range(CHUNK_BLOCKS):
            fetch(chunk * CHUNK_BLOCKS + i).wait()
        keys = kv[pl.ds(chunk * CHUNK_BLOCKS, CHUNK_BLOCKS), :, 0:features].reshape(
            chunk_rows, features
        )
        values = kv[pl.ds(chunk * CHUNK_BLOCKS, CHUNK_BLOCKS), :, features:width].reshape(
            chunk_rows, features
        )
        for g in range(heads):
            scores = lax.dot_general(
                q_ref[:, g * features:(g + 1) * features], keys,
                (((1,), (1,)), ((), ())), preferred_element_type=jnp.float32,
            )
            if masked:
                key_at = chunk * chunk_rows + lax.broadcasted_iota(
                    jnp.int32, scores.shape, 1)
                row_at = own * rows + lax.broadcasted_iota(jnp.int32, scores.shape, 0)
                allowed = key_at <= row_at
                scores = jnp.where(allowed, scores, MASKED)
            before = top[g]
            now = jnp.maximum(before, jnp.max(scores, axis=1, keepdims=True))
            top[g] = now
            weights = jnp.exp2((scores - jnp.tile(now, (1, chunk_rows // features))) * factor)
            if masked:
                weights = jnp.where(allowed, weights, 0.0)
            shrink = jnp.exp2((before - now) * factor)
            total[g] = total[g] * shrink + jnp.sum(weights, axis=1, keepdims=True)
            acc[g] = acc[g] * shrink + jnp.dot(
                weights.astype(jnp.bfloat16), values, preferred_element_type=jnp.float32
            )

    @pl.loop(0, last_chunk)
    def _(chunk):
        step(chunk, False)

    step(last_chunk, True)

    for g in range(heads):
        hidden[:, g * features:(g + 1) * features] = (acc[g] / total[g]).astype(jnp.bfloat16)

    weight_copy.wait()
    part_blocks = blocks // groups
    part_rows = weight_rows // 2
    for t in range(groups):
        term = None
        for half in range(2):
            piece = wt[t * part_blocks:(t + 1) * part_blocks,
                       half * part_rows:(half + 1) * part_rows, :].reshape(
                part_blocks * part_rows, width)
            product = lax.dot_general(
                hidden[:, half * width:(half + 1) * width], piece,
                (((1,), (1,)), ((), ())), preferred_element_type=jnp.float32,
            )
            term = product if term is None else term + product
        out_ref[t] = term.astype(jnp.bfloat16)


def body(placement, queries, keys, values, out_weight):
    rows, columns = queries.shape
    blocks = placement.shape[0]
    heads = columns // HEAD_FEATURES
    groups = lax.axis_size("head")
    width = 2 * HEAD_FEATURES
    turned = out_weight.T
    sent = jnp.concatenate(
        [jnp.concatenate([keys, values], 1), turned[:, :width], turned[:, width:]], 0
    )
    weight_rows = 2 * turned.shape[0]
    gathered = lax.all_gather(sent, "ctx", axis=0)
    out_columns = blocks * turned.shape[0] // groups
    terms = pl.pallas_call(
        functools.partial(attend_kernel, blocks, rows, heads, groups),
        out_shape=jax.ShapeDtypeStruct((groups, rows, out_columns), jnp.bfloat16),
        in_specs=[
            pl.BlockSpec(memory_space=pltpu.SMEM),
            pl.BlockSpec(memory_space=pltpu.VMEM),
            pl.BlockSpec(memory_space=pl.ANY),
        ],
        out_specs=pl.BlockSpec(memory_space=pltpu.VMEM),
        scratch_shapes=[
            pltpu.SMEM((blocks,), jnp.int32),
            pltpu.VMEM((blocks, rows, width), jnp.bfloat16),
            pltpu.VMEM((blocks, weight_rows, width), jnp.bfloat16),
            pltpu.VMEM((heads, rows, HEAD_FEATURES), jnp.float32),
            pltpu.VMEM((heads, rows, HEAD_FEATURES), jnp.float32),
            pltpu.VMEM((heads, rows, HEAD_FEATURES), jnp.float32),
            pltpu.VMEM((rows, columns), jnp.bfloat16),
            pltpu.SemaphoreType.DMA((blocks,)),
            pltpu.SemaphoreType.DMA,
        ],
        compiler_params=pltpu.CompilerParams(vmem_limit_bytes=48 * 1024 * 1024),
        name="attend",
    )(placement, queries, gathered)
    return lax.psum_scatter(
        terms.reshape(groups * rows, out_columns), "head", scatter_dimension=0, tiled=True
    )


def solution(mesh):
    placed = (P(), P("ctx", "head"), P("ctx", "head"), P("ctx", "head"), P("head", "ctx"))
    return jax.shard_map(
        body, mesh=mesh, in_specs=placed, out_specs=P("ctx", "head"), check_vma=False
    )
```

```python
import functools

import jax
import jax.numpy as jnp
from jax import lax
from jax.experimental import pallas as pl
from jax.experimental.pallas import tpu as pltpu
from jax.sharding import PartitionSpec as P

HEAD_FEATURES = 128
MASKED = -1e30
LOG2_E = 1.4426950408889634
FACTOR = HEAD_FEATURES ** (-0.5) * LOG2_E
X_SIZE, Y_SIZE, CORES = 4, 8, 2
PEERS = X_SIZE * CORES
SLOTS = Y_SIZE * CORES
STAT_ROWS = 16


def ctx_of(x, y, core):
    return (x * Y_SIZE + y) * CORES + core


Y_GROUPS = [[ctx_of(x, y, c) for y in range(Y_SIZE)] for x in range(X_SIZE) for c in range(CORES)]
XC_GROUPS = [[ctx_of(x, y, c) for x in range(X_SIZE) for c in range(CORES)] for y in range(Y_SIZE)]


def pack_kernel(key_ref, value_ref, weight_ref, out_ref):
    rows, features = key_ref.shape
    half = rows // 2
    count = weight_ref.shape[0]
    width = out_ref.shape[1]
    out_ref[0:half, 0:features] = key_ref[0:half, :]
    out_ref[0:half, features:width] = key_ref[half:rows, :]
    out_ref[half:rows, :] = value_ref[...].astype(jnp.float32).T.astype(jnp.bfloat16)
    for i in range(2):
        out_ref[rows + i * count:rows + (i + 1) * count, :] = (
            weight_ref[:, i * width:(i + 1) * width])


def attend_kernel(rows, heads, place_ref, q_ref, line_ref, other_ref, out_ref,
                  listed, kv, top, total, acc, kv_sem):
    features = HEAD_FEATURES
    half = rows // 2
    me = lax.axis_index("ctx")
    core = lax.rem(me, CORES)
    y = lax.rem(lax.div(me, CORES), Y_SIZE)
    x = lax.div(me, CORES * Y_SIZE)

    copies = [
        pltpu.make_async_copy(
            line_ref.at[:, pl.ds(0, rows), :], kv.at[pl.ds(0, Y_SIZE)], kv_sem.at[0]),
        pltpu.make_async_copy(other_ref, kv.at[pl.ds(Y_SIZE, Y_SIZE)], kv_sem.at[1]),
    ]
    for copy in copies:
        copy.start()
    for copy in copies:
        copy.wait()

    def step(s, slots, masked):
        keys = jnp.concatenate(
            [kv[slot, 0:half, p * features:(p + 1) * features] for slot in slots for p in (0, 1)], 0)
        values = jnp.concatenate([kv[slot, half:rows, :] for slot in slots], 1)

        def scores_of(t):
            scores = lax.dot_general(
                keys, q_ref[s, :, t * features:(t + 1) * features],
                (((1,), (1,)), ((), ())), preferred_element_type=jnp.float32,
            )
            if masked:
                scores = jnp.where(causal(scores.shape), scores, MASKED)
            return scores

        def causal(shape):
            return (lax.broadcasted_iota(jnp.int32, shape, 0)
                    <= lax.broadcasted_iota(jnp.int32, shape, 1))

        def absorb(t, scores):
            lanes = slice(t * rows, (t + 1) * rows)
            before = top[:, lanes]
            now = jnp.maximum(before, jnp.max(scores, axis=0, keepdims=True))
            top[:, lanes] = now
            weights = jnp.exp2((scores - now[0:1]) * FACTOR)
            if masked:
                weights = jnp.where(causal(scores.shape), weights, 0.0)
            shrink = jnp.exp2((before - now) * FACTOR)
            total[:, lanes] = total[:, lanes] * shrink + jnp.sum(weights, axis=0, keepdims=True)
            acc[:, lanes] = acc[:, lanes] * shrink[0:1] + jnp.dot(
                values, weights.astype(jnp.bfloat16), preferred_element_type=jnp.float32)

        scores = scores_of(0)
        for t in range(heads):
            following = scores_of(t + 1) if t + 1 < heads else None
            absorb(t, scores)
            scores = following

    @pl.loop(0, PEERS)
    def _(s):
        query_x = lax.div(s, CORES)
        query_core = lax.rem(s, CORES)
        query_at = place_ref[ctx_of(query_x, y, query_core)]

        def note(i, found):
            slot_core = jnp.where(i < Y_SIZE, core, 1 - core)
            key_at = place_ref[ctx_of(x, lax.rem(i, Y_SIZE), slot_core)]
            listed[found] = i
            return found + (key_at < query_at).astype(jnp.int32)

        found = lax.fori_loop(0, SLOTS, note, jnp.int32(0))
        top[...] = jnp.full_like(top, MASKED)
        total[...] = jnp.zeros_like(total)
        acc[...] = jnp.zeros_like(acc)

        @pl.when(query_x == x)
        def _():
            step(s, [jnp.where(query_core == core, y, Y_SIZE + y)], True)

        fours = lax.div(found, 4)

        @pl.loop(0, fours)
        def _(i):
            step(s, [listed[4 * i + j] for j in range(4)], False)

        rest = found - 4 * fours

        @pl.when(rest >= 2)
        def _():
            step(s, [listed[4 * fours], listed[4 * fours + 1]], False)

        @pl.when(lax.rem(rest, 2) == 1)
        def _():
            step(s, [listed[found - 1]], False)

        row = lax.broadcasted_iota(jnp.int32, (STAT_ROWS, rows), 0)
        stats = jnp.zeros((STAT_ROWS, rows), jnp.float32)
        for t in range(heads):
            lanes = slice(t * rows, (t + 1) * rows)
            norm = jnp.maximum(total[0:1, lanes], 1e-30)
            out_ref[s, t * features:(t + 1) * features, :] = (
                acc[:, lanes] * (1.0 / norm)).astype(jnp.bfloat16)
            left = top[0:1, lanes] * FACTOR + jnp.log(norm) * LOG2_E
            for part in range(3):
                piece = left.astype(jnp.bfloat16).astype(jnp.float32)
                stats = jnp.where(row == 3 * t + part, piece, stats)
                left = left - piece
        out_ref[s, heads * features:heads * features + STAT_ROWS, :] = stats.astype(jnp.bfloat16)


def merge_kernel(heads, groups, part_ref, weight_ref, out_ref, hidden, weight, sems):
    features = HEAD_FEATURES
    width = 2 * features
    copies = [
        pltpu.make_async_copy(
            weight_ref.at[x * CORES + c], weight.at[x, :, c], sems.at[x * CORES + c])
        for x in range(X_SIZE) for c in range(CORES)
    ]
    for copy in copies:
        copy.start()

    stats = [
        part_ref[j, heads * features:heads * features + STAT_ROWS, :].astype(jnp.float32)
        for j in range(PEERS)
    ]
    for c in range(CORES):
        for t in range(heads):
            peers = [i * CORES + c for i in range(X_SIZE)]
            levels = [
                stats[j][3 * t:3 * t + 1] + stats[j][3 * t + 1:3 * t + 2]
                + stats[j][3 * t + 2:3 * t + 3]
                for j in peers
            ]
            peak = functools.reduce(jnp.maximum, levels)
            shares = [jnp.exp2(level - peak) for level in levels]
            inverse = 1.0 / sum(shares)
            merged = sum(
                part_ref[j, t * features:(t + 1) * features, :].astype(jnp.float32)
                * (share * inverse)
                for j, share in zip(peers, shares)
            )
            at = (c * heads + t) * features
            hidden[:, at:at + features] = merged.T.astype(jnp.bfloat16)

    for copy in copies:
        copy.wait()
    lines = X_SIZE * Y_SIZE // groups
    parts = Y_SIZE // lines
    part_rows = weight.shape[3] // 2
    for g in range(groups):
        term = None
        for side in range(2):
            start = (g % parts) * lines
            piece = weight[g // parts, start:start + lines, :,
                           side * part_rows:(side + 1) * part_rows, :].reshape(
                lines * CORES * part_rows, width)
            product = lax.dot_general(
                hidden[:, side * width:(side + 1) * width], piece,
                (((1,), (1,)), ((), ())), preferred_element_type=jnp.float32,
            )
            term = product if term is None else term + product
        out_ref[g] = term.astype(jnp.bfloat16)


def hold(array):
    return pl.pallas_call(
        lambda array_ref, out_ref: None,
        out_shape=jax.ShapeDtypeStruct(array.shape, array.dtype),
        in_specs=[pl.BlockSpec(memory_space=pl.ANY)],
        out_specs=pl.BlockSpec(memory_space=pl.ANY),
        input_output_aliases={0: 0},
        name="hold",
    )(array)


def body(placement, queries, keys, values, out_weight):
    rows, columns = queries.shape
    blocks = placement.shape[0]
    width = 2 * HEAD_FEATURES
    heads = columns // HEAD_FEATURES // CORES
    groups = lax.axis_size("head")

    turned = out_weight.T
    sent = pl.pallas_call(
        pack_kernel,
        out_shape=jax.ShapeDtypeStruct((rows + 2 * turned.shape[0], width), jnp.bfloat16),
        in_specs=[pl.BlockSpec(memory_space=pltpu.VMEM)] * 3,
        out_specs=pl.BlockSpec(memory_space=pltpu.VMEM),
        name="pack",
    )(keys, values, turned)
    line = lax.all_gather(sent, "ctx", axis=0, axis_index_groups=Y_GROUPS)

    asked = jnp.stack([queries[:, c * width:(c + 1) * width] for c in range(CORES)], 0)
    asked = jnp.broadcast_to(asked[None], (X_SIZE,) + asked.shape).reshape(PEERS, rows, width)
    asked = lax.all_to_all(asked, "ctx", 0, 0, tiled=True, axis_index_groups=XC_GROUPS)
    asked = hold(asked)
    other = lax.ppermute(line[:, :rows], "ctx", [(i, i ^ 1) for i in range(blocks)])
    weights = lax.all_gather(line[:, rows:], "ctx", axis=0, axis_index_groups=XC_GROUPS)

    parts = pl.pallas_call(
        functools.partial(attend_kernel, rows, heads),
        out_shape=jax.ShapeDtypeStruct((PEERS, width + STAT_ROWS, rows), jnp.bfloat16),
        in_specs=[
            pl.BlockSpec(memory_space=pltpu.SMEM),
            pl.BlockSpec(memory_space=pltpu.VMEM),
            pl.BlockSpec(memory_space=pl.ANY),
            pl.BlockSpec(memory_space=pl.ANY),
        ],
        out_specs=pl.BlockSpec(memory_space=pltpu.VMEM),
        scratch_shapes=[
            pltpu.SMEM((SLOTS + 1,), jnp.int32),
            pltpu.VMEM((SLOTS, rows, width), jnp.bfloat16),
            pltpu.VMEM((8, heads * rows), jnp.float32),
            pltpu.VMEM((8, heads * rows), jnp.float32),
            pltpu.VMEM((HEAD_FEATURES, heads * rows), jnp.float32),
            pltpu.SemaphoreType.DMA((2,)),
        ],
        compiler_params=pltpu.CompilerParams(
            vmem_limit_bytes=32 * 1024 * 1024),
        cost_estimate=pl.CostEstimate(
            flops=9_000_000_000, transcendentals=9_000_000, bytes_accessed=5_000_000),
        name="attend",
    )(placement, asked, line, other)

    gathered = lax.all_to_all(parts, "ctx", 0, 0, tiled=True, axis_index_groups=XC_GROUPS)

    out_columns = blocks * turned.shape[0] // groups
    weight_shape = (X_SIZE, Y_SIZE, CORES) + (2 * turned.shape[0], width)
    terms = pl.pallas_call(
        functools.partial(merge_kernel, heads, groups),
        out_shape=jax.ShapeDtypeStruct((groups, rows, out_columns), jnp.bfloat16),
        in_specs=[
            pl.BlockSpec(memory_space=pltpu.VMEM),
            pl.BlockSpec(memory_space=pl.ANY),
        ],
        out_specs=pl.BlockSpec(memory_space=pltpu.VMEM),
        scratch_shapes=[
            pltpu.VMEM((rows, columns), jnp.bfloat16),
            pltpu.VMEM(weight_shape, jnp.bfloat16),
            pltpu.SemaphoreType.DMA((PEERS,)),
        ],
        compiler_params=pltpu.CompilerParams(vmem_limit_bytes=32 * 1024 * 1024),
        name="merge_project",
    )(gathered, weights)
    return lax.psum_scatter(
        terms.reshape(groups * rows, out_columns), "head", scatter_dimension=0, tiled=True
    )


def solution(mesh):
    placed = (P(), P("ctx", "head"), P("ctx", "head"), P("ctx", "head"), P("head", "ctx"))

    return jax.shard_map(
        body, mesh=mesh, in_specs=placed, out_specs=P("ctx", "head"), check_vma=False
    )
```

```python
import functools

import jax
import jax.numpy as jnp
from jax import lax
from jax.experimental import pallas as pl
from jax.experimental.pallas import tpu as pltpu
from jax.sharding import PartitionSpec as P

HEAD_FEATURES = 128
MASKED = -1e30
LOG2_E = 1.4426950408889634
FACTOR = HEAD_FEATURES ** (-0.5) * LOG2_E
X_SIZE, Y_SIZE, CORES = 4, 8, 2
PEERS = X_SIZE * CORES
SLOTS = Y_SIZE * CORES
STAT_ROWS = 16


def ctx_of(x, y, core):
    return (x * Y_SIZE + y) * CORES + core


Y_GROUPS = [[ctx_of(x, y, c) for y in range(Y_SIZE)] for x in range(X_SIZE) for c in range(CORES)]
XC_GROUPS = [[ctx_of(x, y, c) for x in range(X_SIZE) for c in range(CORES)] for y in range(Y_SIZE)]


def pack_kernel(key_ref, value_ref, query_ref, weight_ref, line_ref, ask_ref, column_ref):
    rows, features = key_ref.shape
    half = rows // 2
    count = weight_ref.shape[0]
    width = line_ref.shape[1]
    line_ref[0:half, 0:features] = key_ref[0:half, :]
    line_ref[0:half, features:width] = key_ref[half:rows, :]
    line_ref[half:rows, :] = value_ref[...].astype(jnp.float32).T.astype(jnp.bfloat16)
    for c in range(CORES):
        piece = query_ref[:, c * width:(c + 1) * width]
        for x in range(X_SIZE):
            ask_ref[x * CORES + c] = piece
    for i in range(2):
        piece = weight_ref[:, i * width:(i + 1) * width]
        for y in range(Y_SIZE):
            column_ref[y, i * count:(i + 1) * count, :] = piece


def attend_kernel(rows, heads, place_ref, ask_ref, line_ref, other_ref, out_ref,
                  listed, q_ref, kv, top, total, acc, kv_sem):
    features = HEAD_FEATURES
    half = rows // 2
    me = lax.axis_index("ctx")
    core = lax.rem(me, CORES)
    y = lax.rem(lax.div(me, CORES), Y_SIZE)
    x = lax.div(me, CORES * Y_SIZE)

    copies = [
        pltpu.make_async_copy(line_ref, kv.at[pl.ds(0, Y_SIZE)], kv_sem.at[0]),
        pltpu.make_async_copy(other_ref, kv.at[pl.ds(Y_SIZE, Y_SIZE)], kv_sem.at[1]),
        pltpu.make_async_copy(ask_ref, q_ref, kv_sem.at[2]),
    ]
    for copy in copies:
        copy.start()
    for copy in copies:
        copy.wait()

    def step(s, slots, masked):
        keys = jnp.concatenate(
            [kv[slot, 0:half, p * features:(p + 1) * features] for slot in slots for p in (0, 1)], 0)
        values = jnp.concatenate([kv[slot, half:rows, :] for slot in slots], 1)

        def scores_of(t):
            scores = lax.dot_general(
                keys, q_ref[s, :, t * features:(t + 1) * features],
                (((1,), (1,)), ((), ())), preferred_element_type=jnp.float32,
            )
            if masked:
                scores = jnp.where(causal(scores.shape), scores, MASKED)
            return scores

        def causal(shape):
            return (lax.broadcasted_iota(jnp.int32, shape, 0)
                    <= lax.broadcasted_iota(jnp.int32, shape, 1))

        def absorb(t, scores):
            lanes = slice(t * rows, (t + 1) * rows)
            before = top[:, lanes]
            now = jnp.maximum(before, jnp.max(scores, axis=0, keepdims=True))
            top[:, lanes] = now
            weights = jnp.exp2((scores - now[0:1]) * FACTOR)
            if masked:
                weights = jnp.where(causal(scores.shape), weights, 0.0)
            shrink = jnp.exp2((before - now) * FACTOR)
            total[:, lanes] = total[:, lanes] * shrink + jnp.sum(weights, axis=0, keepdims=True)
            acc[:, lanes] = acc[:, lanes] * shrink[0:1] + jnp.dot(
                values, weights.astype(jnp.bfloat16), preferred_element_type=jnp.float32)

        scores = scores_of(0)
        for t in range(heads):
            following = scores_of(t + 1) if t + 1 < heads else None
            absorb(t, scores)
            scores = following

    @pl.loop(0, PEERS)
    def _(s):
        query_x = lax.div(s, CORES)
        query_core = lax.rem(s, CORES)
        query_at = place_ref[ctx_of(query_x, y, query_core)]

        def note(i, found):
            slot_core = jnp.where(i < Y_SIZE, core, 1 - core)
            key_at = place_ref[ctx_of(x, lax.rem(i, Y_SIZE), slot_core)]
            listed[found] = i
            return found + (key_at < query_at).astype(jnp.int32)

        found = lax.fori_loop(0, SLOTS, note, jnp.int32(0))
        top[...] = jnp.full_like(top, MASKED)
        total[...] = jnp.zeros_like(total)
        acc[...] = jnp.zeros_like(acc)

        @pl.when(query_x == x)
        def _():
            step(s, [jnp.where(query_core == core, y, Y_SIZE + y)], True)

        fours = lax.div(found, 4)

        @pl.loop(0, fours)
        def _(i):
            step(s, [listed[4 * i + j] for j in range(4)], False)

        rest = found - 4 * fours

        @pl.when(rest >= 2)
        def _():
            step(s, [listed[4 * fours], listed[4 * fours + 1]], False)

        @pl.when(lax.rem(rest, 2) == 1)
        def _():
            step(s, [listed[found - 1]], False)

        row = lax.broadcasted_iota(jnp.int32, (STAT_ROWS, rows), 0)
        stats = jnp.zeros((STAT_ROWS, rows), jnp.float32)
        for t in range(heads):
            lanes = slice(t * rows, (t + 1) * rows)
            norm = jnp.maximum(total[0:1, lanes], 1e-30)
            out_ref[s, t * features:(t + 1) * features, :] = (
                acc[:, lanes] * (1.0 / norm)).astype(jnp.bfloat16)
            left = top[0:1, lanes] * FACTOR + jnp.log(norm) * LOG2_E
            for part in range(3):
                piece = left.astype(jnp.bfloat16).astype(jnp.float32)
                stats = jnp.where(row == 3 * t + part, piece, stats)
                left = left - piece
        out_ref[s, heads * features:heads * features + STAT_ROWS, :] = stats.astype(jnp.bfloat16)


def merge_kernel(heads, groups, part_ref, weight_ref, out_ref, hidden, weight, sems):
    features = HEAD_FEATURES
    width = 2 * features
    copies = [
        pltpu.make_async_copy(
            weight_ref.at[x * CORES + c], weight.at[x, :, c], sems.at[x * CORES + c])
        for x in range(X_SIZE) for c in range(CORES)
    ]
    for copy in copies:
        copy.start()

    stats = [
        part_ref[j, heads * features:heads * features + STAT_ROWS, :].astype(jnp.float32)
        for j in range(PEERS)
    ]
    for c in range(CORES):
        for t in range(heads):
            peers = [i * CORES + c for i in range(X_SIZE)]
            levels = [
                stats[j][3 * t:3 * t + 1] + stats[j][3 * t + 1:3 * t + 2]
                + stats[j][3 * t + 2:3 * t + 3]
                for j in peers
            ]
            peak = functools.reduce(jnp.maximum, levels)
            shares = [jnp.exp2(level - peak) for level in levels]
            inverse = 1.0 / sum(shares)
            merged = sum(
                part_ref[j, t * features:(t + 1) * features, :].astype(jnp.float32)
                * (share * inverse)
                for j, share in zip(peers, shares)
            )
            at = (c * heads + t) * features
            hidden[:, at:at + features] = merged.T.astype(jnp.bfloat16)

    for copy in copies:
        copy.wait()
    lines = X_SIZE * Y_SIZE // groups
    parts = Y_SIZE // lines
    part_rows = weight.shape[3] // 2
    for g in range(groups):
        term = None
        for side in range(2):
            start = (g % parts) * lines
            piece = weight[g // parts, start:start + lines, :,
                           side * part_rows:(side + 1) * part_rows, :].reshape(
                lines * CORES * part_rows, width)
            product = lax.dot_general(
                hidden[:, side * width:(side + 1) * width], piece,
                (((1,), (1,)), ((), ())), preferred_element_type=jnp.float32,
            )
            term = product if term is None else term + product
        out_ref[g] = term.astype(jnp.bfloat16)


def hold(array):
    return pl.pallas_call(
        lambda array_ref, out_ref: None,
        out_shape=jax.ShapeDtypeStruct(array.shape, array.dtype),
        in_specs=[pl.BlockSpec(memory_space=pl.ANY)],
        out_specs=pl.BlockSpec(memory_space=pl.ANY),
        input_output_aliases={0: 0},
        name="hold",
    )(array)


def body(placement, queries, keys, values, out_weight):
    rows, columns = queries.shape
    blocks = placement.shape[0]
    width = 2 * HEAD_FEATURES
    heads = columns // HEAD_FEATURES // CORES
    groups = lax.axis_size("head")

    turned = out_weight.T
    sent, asked, column = pl.pallas_call(
        pack_kernel,
        out_shape=(
            jax.ShapeDtypeStruct((rows, width), jnp.bfloat16),
            jax.ShapeDtypeStruct((PEERS, rows, width), jnp.bfloat16),
            jax.ShapeDtypeStruct((Y_SIZE, 2 * turned.shape[0], width), jnp.bfloat16),
        ),
        in_specs=[pl.BlockSpec(memory_space=pltpu.VMEM)] * 4,
        out_specs=(pl.BlockSpec(memory_space=pltpu.VMEM),) * 3,
        name="pack",
    )(keys, values, queries, turned)
    line = lax.all_gather(sent, "ctx", axis=0, axis_index_groups=Y_GROUPS)

    column = lax.all_to_all(column, "ctx", 0, 0, tiled=True, axis_index_groups=Y_GROUPS)
    column = hold(column)
    asked = lax.all_to_all(asked, "ctx", 0, 0, tiled=True, axis_index_groups=XC_GROUPS)
    asked = hold(asked)
    other = lax.ppermute(line, "ctx", [(i, i ^ 1) for i in range(blocks)])
    weights = lax.all_gather(column, "ctx", axis=0, axis_index_groups=XC_GROUPS)

    parts = pl.pallas_call(
        functools.partial(attend_kernel, rows, heads),
        out_shape=jax.ShapeDtypeStruct((PEERS, width + STAT_ROWS, rows), jnp.bfloat16),
        in_specs=[
            pl.BlockSpec(memory_space=pltpu.SMEM),
            pl.BlockSpec(memory_space=pl.ANY),
            pl.BlockSpec(memory_space=pl.ANY),
            pl.BlockSpec(memory_space=pl.ANY),
        ],
        out_specs=pl.BlockSpec(memory_space=pltpu.VMEM),
        scratch_shapes=[
            pltpu.SMEM((SLOTS + 1,), jnp.int32),
            pltpu.VMEM((PEERS, rows, width), jnp.bfloat16),
            pltpu.VMEM((SLOTS, rows, width), jnp.bfloat16),
            pltpu.VMEM((8, heads * rows), jnp.float32),
            pltpu.VMEM((8, heads * rows), jnp.float32),
            pltpu.VMEM((HEAD_FEATURES, heads * rows), jnp.float32),
            pltpu.SemaphoreType.DMA((3,)),
        ],
        compiler_params=pltpu.CompilerParams(
            vmem_limit_bytes=60 * 1024 * 1024),
        cost_estimate=pl.CostEstimate(
            flops=9_000_000_000, transcendentals=9_000_000, bytes_accessed=5_000_000),
        name="attend",
    )(placement, asked, line, other)

    gathered = lax.all_to_all(parts, "ctx", 0, 0, tiled=True, axis_index_groups=XC_GROUPS)

    out_columns = blocks * turned.shape[0] // groups
    weight_shape = (X_SIZE, Y_SIZE, CORES) + (2 * turned.shape[0], width)
    terms = pl.pallas_call(
        functools.partial(merge_kernel, heads, groups),
        out_shape=jax.ShapeDtypeStruct((groups, rows, out_columns), jnp.bfloat16),
        in_specs=[
            pl.BlockSpec(memory_space=pltpu.VMEM),
            pl.BlockSpec(memory_space=pl.ANY),
        ],
        out_specs=pl.BlockSpec(memory_space=pltpu.VMEM),
        scratch_shapes=[
            pltpu.VMEM((rows, columns), jnp.bfloat16),
            pltpu.VMEM(weight_shape, jnp.bfloat16),
            pltpu.SemaphoreType.DMA((PEERS,)),
        ],
        compiler_params=pltpu.CompilerParams(vmem_limit_bytes=60 * 1024 * 1024),
        name="merge_project",
    )(gathered, weights)
    return lax.psum_scatter(
        terms.reshape(groups * rows, out_columns), "head", scatter_dimension=0, tiled=True
    )


def solution(mesh):
    placed = (P(), P("ctx", "head"), P("ctx", "head"), P("ctx", "head"), P("head", "ctx"))

    return jax.shard_map(
        body, mesh=mesh, in_specs=placed, out_specs=P("ctx", "head"), check_vma=False
    )
```

```python
import functools

import jax
import jax.numpy as jnp
from jax import lax
from jax.experimental import pallas as pl
from jax.experimental.pallas import tpu as pltpu
from jax.sharding import PartitionSpec as P

HEAD_FEATURES = 128
MASKED = -1e30
LOG2_E = 1.4426950408889634
FACTOR = HEAD_FEATURES ** (-0.5) * LOG2_E
X_SIZE, Y_SIZE, CORES = 4, 8, 2
PEERS = X_SIZE * CORES
SLOTS = Y_SIZE * CORES
STAT_ROWS = 16


def ctx_of(x, y, core):
    return (x * Y_SIZE + y) * CORES + core


Y_GROUPS = [[ctx_of(x, y, c) for y in range(Y_SIZE)] for x in range(X_SIZE) for c in range(CORES)]
XC_GROUPS = [[ctx_of(x, y, c) for x in range(X_SIZE) for c in range(CORES)] for y in range(Y_SIZE)]


def pack_kernel(key_ref, value_ref, weight_ref, out_ref):
    rows, features = key_ref.shape
    half = rows // 2
    count = weight_ref.shape[0]
    width = out_ref.shape[1]
    out_ref[0:half, 0:features] = key_ref[0:half, :]
    out_ref[0:half, features:width] = key_ref[half:rows, :]
    out_ref[half:rows, :] = value_ref[...].astype(jnp.float32).T.astype(jnp.bfloat16)
    for i in range(2):
        out_ref[rows + i * count:rows + (i + 1) * count, :] = (
            weight_ref[:, i * width:(i + 1) * width])


def attend_kernel(own, rows, heads, place_ref, q_ref, line_ref, other_ref, out_ref,
                  listed, kv, top, total, acc, kv_sem):
    features = HEAD_FEATURES
    half = rows // 2
    me = lax.axis_index("ctx")
    core = lax.rem(me, CORES)
    y = lax.rem(lax.div(me, CORES), Y_SIZE)
    x = lax.div(me, CORES * Y_SIZE)

    copies = [
        pltpu.make_async_copy(
            line_ref.at[:, pl.ds(0, rows), :], kv.at[pl.ds(0, Y_SIZE)], kv_sem.at[0]),
        pltpu.make_async_copy(
            other_ref.at[:, pl.ds(0, rows), :], kv.at[pl.ds(Y_SIZE, Y_SIZE)], kv_sem.at[1]),
    ]
    for copy in copies:
        copy.start()
    for copy in copies:
        copy.wait()

    def step(s, slots, masked):
        keys = jnp.concatenate(
            [kv[slot, 0:half, p * features:(p + 1) * features] for slot in slots for p in (0, 1)], 0)
        values = jnp.concatenate([kv[slot, half:rows, :] for slot in slots], 1)

        def scores_of(t):
            scores = lax.dot_general(
                keys, q_ref[s, :, t * features:(t + 1) * features],
                (((1,), (1,)), ((), ())), preferred_element_type=jnp.float32,
            )
            if masked:
                scores = jnp.where(causal(scores.shape), scores, MASKED)
            return scores

        def causal(shape):
            return (lax.broadcasted_iota(jnp.int32, shape, 0)
                    <= lax.broadcasted_iota(jnp.int32, shape, 1))

        def absorb(t, scores):
            lanes = slice(t * rows, (t + 1) * rows)
            before = top[:, lanes]
            now = jnp.maximum(before, jnp.max(scores, axis=0, keepdims=True))
            top[:, lanes] = now
            weights = jnp.exp2((scores - now[0:1]) * FACTOR)
            if masked:
                weights = jnp.where(causal(scores.shape), weights, 0.0)
            shrink = jnp.exp2((before - now) * FACTOR)
            total[:, lanes] = total[:, lanes] * shrink + jnp.sum(weights, axis=0, keepdims=True)
            acc[:, lanes] = acc[:, lanes] * shrink[0:1] + jnp.dot(
                values, weights.astype(jnp.bfloat16), preferred_element_type=jnp.float32)

        scores = scores_of(0)
        for t in range(heads):
            following = scores_of(t + 1) if t + 1 < heads else None
            absorb(t, scores)
            scores = following

    @pl.loop(0, CORES if own else PEERS - CORES)
    def _(i):
        turn = lax.div(i, CORES) + (0 if own else 1)
        query_x = lax.rem(x + turn, X_SIZE)
        query_core = lax.rem(i + core, CORES)
        s = query_x * CORES + query_core
        slot = i if own else s
        query_at = place_ref[ctx_of(query_x, y, query_core)]

        def note(i, found):
            slot_core = jnp.where(i < Y_SIZE, core, 1 - core)
            key_at = place_ref[ctx_of(x, lax.rem(i, Y_SIZE), slot_core)]
            listed[found] = i
            return found + (key_at < query_at).astype(jnp.int32)

        found = lax.fori_loop(0, SLOTS, note, jnp.int32(0))
        top[...] = jnp.full_like(top, MASKED)
        total[...] = jnp.zeros_like(total)
        acc[...] = jnp.zeros_like(acc)

        if own:
            step(s, [jnp.where(query_core == core, y, Y_SIZE + y)], True)

        fours = lax.div(found, 4)

        @pl.loop(0, fours)
        def _(i):
            step(s, [listed[4 * i + j] for j in range(4)], False)

        rest = found - 4 * fours

        @pl.when(rest >= 2)
        def _():
            step(s, [listed[4 * fours], listed[4 * fours + 1]], False)

        @pl.when(lax.rem(rest, 2) == 1)
        def _():
            step(s, [listed[found - 1]], False)

        row = lax.broadcasted_iota(jnp.int32, (STAT_ROWS, rows), 0)
        stats = jnp.zeros((STAT_ROWS, rows), jnp.float32)
        for t in range(heads):
            lanes = slice(t * rows, (t + 1) * rows)
            norm = jnp.maximum(total[0:1, lanes], 1e-30)
            out_ref[slot, t * features:(t + 1) * features, :] = (
                acc[:, lanes] * (1.0 / norm)).astype(jnp.bfloat16)
            left = top[0:1, lanes] * FACTOR + jnp.log(norm) * LOG2_E
            for part in range(3):
                piece = left.astype(jnp.bfloat16).astype(jnp.float32)
                stats = jnp.where(row == 3 * t + part, piece, stats)
                left = left - piece
        out_ref[slot, heads * features:heads * features + STAT_ROWS, :] = stats.astype(jnp.bfloat16)


def merge_kernel(heads, groups, part_ref, own_ref, mate_ref, weight_ref, out_ref,
                 hidden, chip, weight, sems):
    features = HEAD_FEATURES
    width = 2 * features
    me = lax.axis_index("ctx")
    core = lax.rem(me, CORES)
    x = lax.div(me, CORES * Y_SIZE)
    copies = [
        pltpu.make_async_copy(weight_ref.at[j], weight.at[j], sems.at[j]) for j in range(PEERS)
    ]
    for copy in copies:
        copy.start()
    chip[core] = own_ref[0]
    chip[1 - core] = mate_ref[0]

    for c in range(CORES):
        sources = [chip.at[c]] + [
            part_ref.at[lax.rem(x + turn, X_SIZE) * CORES + c] for turn in range(1, X_SIZE)
        ]
        stats = [
            source[heads * features:heads * features + STAT_ROWS, :].astype(jnp.float32)
            for source in sources
        ]
        for t in range(heads):
            levels = [
                stat[3 * t:3 * t + 1] + stat[3 * t + 1:3 * t + 2] + stat[3 * t + 2:3 * t + 3]
                for stat in stats
            ]
            peak = functools.reduce(jnp.maximum, levels)
            shares = [jnp.exp2(level - peak) for level in levels]
            inverse = 1.0 / sum(shares)
            merged = sum(
                source[t * features:(t + 1) * features, :].astype(jnp.float32)
                * (share * inverse)
                for source, share in zip(sources, shares)
            )
            at = (c * heads + t) * features
            hidden[:, at:at + features] = merged.T.astype(jnp.bfloat16)

    lines = X_SIZE * Y_SIZE // groups
    parts = Y_SIZE // lines
    part_rows = weight.shape[2] // 2
    for g in range(groups):
        if g % parts == 0:
            for c in range(CORES):
                copies[(g // parts) * CORES + c].wait()
        term = None
        for side in range(2):
            start = (g % parts) * lines
            piece = jnp.concatenate([
                weight[(g // parts) * CORES + c, start + line,
                           side * part_rows:(side + 1) * part_rows, :]
                for line in range(lines) for c in range(CORES)
            ], 0)
            product = lax.dot_general(
                hidden[:, side * width:(side + 1) * width], piece,
                (((1,), (1,)), ((), ())), preferred_element_type=jnp.float32,
            )
            term = product if term is None else term + product
        out_ref[g] = term.astype(jnp.bfloat16)


def hold(array):
    return pl.pallas_call(
        lambda array_ref, out_ref: None,
        out_shape=jax.ShapeDtypeStruct(array.shape, array.dtype),
        in_specs=[pl.BlockSpec(memory_space=pl.ANY)],
        out_specs=pl.BlockSpec(memory_space=pl.ANY),
        input_output_aliases={0: 0},
        name="hold",
    )(array)


def body(placement, queries, keys, values, out_weight):
    rows, columns = queries.shape
    blocks = placement.shape[0]
    width = 2 * HEAD_FEATURES
    heads = columns // HEAD_FEATURES // CORES
    groups = lax.axis_size("head")

    turned = out_weight.T
    sent = pl.pallas_call(
        pack_kernel,
        out_shape=jax.ShapeDtypeStruct((rows + 2 * turned.shape[0], width), jnp.bfloat16),
        in_specs=[pl.BlockSpec(memory_space=pltpu.VMEM)] * 3,
        out_specs=pl.BlockSpec(memory_space=pltpu.VMEM),
        name="pack",
    )(keys, values, turned)
    line = lax.all_gather(sent, "ctx", axis=0, axis_index_groups=Y_GROUPS)

    asked = jnp.stack([queries[:, c * width:(c + 1) * width] for c in range(CORES)], 0)
    asked = jnp.broadcast_to(asked[None], (X_SIZE,) + asked.shape).reshape(PEERS, rows, width)
    asked = lax.all_to_all(asked, "ctx", 0, 0, tiled=True, axis_index_groups=XC_GROUPS)
    asked = hold(asked)
    swap = [(i, i ^ 1) for i in range(blocks)]
    other = lax.ppermute(line, "ctx", swap)
    spread = line[:, rows:]
    weights = lax.all_gather(spread, "ctx", axis=0, axis_index_groups=XC_GROUPS)

    def attend(own):
        count = CORES if own else PEERS
        return pl.pallas_call(
            functools.partial(attend_kernel, own, rows, heads),
            out_shape=jax.ShapeDtypeStruct((count, width + STAT_ROWS, rows), jnp.bfloat16),
            in_specs=[
                pl.BlockSpec(memory_space=pltpu.SMEM),
                pl.BlockSpec(memory_space=pltpu.VMEM),
                pl.BlockSpec(memory_space=pl.ANY),
                pl.BlockSpec(memory_space=pl.ANY),
            ],
            out_specs=pl.BlockSpec(memory_space=pltpu.VMEM),
            scratch_shapes=[
                pltpu.SMEM((SLOTS + 1,), jnp.int32),
                pltpu.VMEM((SLOTS, rows, width), jnp.bfloat16),
                pltpu.VMEM((8, heads * rows), jnp.float32),
                pltpu.VMEM((8, heads * rows), jnp.float32),
                pltpu.VMEM((HEAD_FEATURES, heads * rows), jnp.float32),
                pltpu.SemaphoreType.DMA((2,)),
            ],
            compiler_params=pltpu.CompilerParams(
                vmem_limit_bytes=32 * 1024 * 1024),
            cost_estimate=pl.CostEstimate(
                flops=1_000_000_000 * count, transcendentals=1_000_000 * count,
                bytes_accessed=5_000_000),
        )(placement, asked, line, other)

    parts = attend(False)
    gathered = lax.all_to_all(parts, "ctx", 0, 0, tiled=True, axis_index_groups=XC_GROUPS)
    near = attend(True)
    mate = lax.ppermute(near[1:], "ctx", swap)

    out_columns = blocks * turned.shape[0] // groups
    terms = pl.pallas_call(
        functools.partial(merge_kernel, heads, groups),
        out_shape=jax.ShapeDtypeStruct((groups, rows, out_columns), jnp.bfloat16),
        in_specs=[
            pl.BlockSpec(memory_space=pltpu.VMEM),
        ] * 3 + [pl.BlockSpec(memory_space=pl.ANY)],
        out_specs=pl.BlockSpec(memory_space=pltpu.VMEM),
        scratch_shapes=[
            pltpu.VMEM((rows, columns), jnp.bfloat16),
            pltpu.VMEM((CORES, width + STAT_ROWS, rows), jnp.bfloat16),
            pltpu.VMEM(weights.shape, jnp.bfloat16),
            pltpu.SemaphoreType.DMA((PEERS,)),
        ],
        compiler_params=pltpu.CompilerParams(vmem_limit_bytes=60 * 1024 * 1024),
        name="merge_project",
    )(gathered, near, mate, weights)
    return lax.psum_scatter(
        terms.reshape(groups * rows, out_columns), "head", scatter_dimension=0, tiled=True
    )


def solution(mesh):
    placed = (P(), P("ctx", "head"), P("ctx", "head"), P("ctx", "head"), P("head", "ctx"))

    return jax.shard_map(
        body, mesh=mesh, in_specs=placed, out_specs=P("ctx", "head"), check_vma=False
    )
```

```python
import functools

import jax
import jax.numpy as jnp
from jax import lax
from jax.experimental import pallas as pl
from jax.experimental.pallas import tpu as pltpu
from jax.sharding import PartitionSpec as P

HEAD_FEATURES = 128
MASKED = -1e30
LOG2_E = 1.4426950408889634
FACTOR = HEAD_FEATURES ** (-0.5) * LOG2_E
X_SIZE, Y_SIZE, CORES = 4, 8, 2
PEERS = X_SIZE * CORES
SLOTS = Y_SIZE * CORES
STAT_ROWS = 16


def ctx_of(x, y, core):
    return (x * Y_SIZE + y) * CORES + core


Y_GROUPS = [[ctx_of(x, y, c) for y in range(Y_SIZE)] for x in range(X_SIZE) for c in range(CORES)]
XC_GROUPS = [[ctx_of(x, y, c) for x in range(X_SIZE) for c in range(CORES)] for y in range(Y_SIZE)]


def pack_kernel(key_ref, value_ref, weight_ref, out_ref):
    rows, features = key_ref.shape
    half = rows // 2
    count = weight_ref.shape[0]
    width = out_ref.shape[1]
    out_ref[0:half, 0:features] = key_ref[0:half, :]
    out_ref[0:half, features:width] = key_ref[half:rows, :]
    out_ref[half:rows, :] = value_ref[...].astype(jnp.float32).T.astype(jnp.bfloat16)
    for i in range(2):
        out_ref[rows + i * count:rows + (i + 1) * count, :] = (
            weight_ref[:, i * width:(i + 1) * width])


def attend_kernel(own, rows, heads, place_ref, ask_ref, *refs):
    features = HEAD_FEATURES
    half = rows // 2
    me = lax.axis_index("ctx")
    core = lax.rem(me, CORES)
    y = lax.rem(lax.div(me, CORES), Y_SIZE)
    x = lax.div(me, CORES * Y_SIZE)

    if own:
        kept_ref, out_ref, listed, q_ref, kv, top, total, acc, kv_sem = refs
        copies = [pltpu.make_async_copy(kept_ref, kv, kv_sem.at[0])]
    else:
        line_ref, other_ref, out_ref, kept_ref, listed, q_ref, kv, top, total, acc, kv_sem = refs
        copies = [
            pltpu.make_async_copy(
                line_ref.at[:, pl.ds(0, rows), :], kv.at[pl.ds(0, Y_SIZE)], kv_sem.at[0]),
            pltpu.make_async_copy(
                other_ref.at[:, pl.ds(0, rows), :], kv.at[pl.ds(Y_SIZE, Y_SIZE)], kv_sem.at[1]),
        ]
    copies.append(pltpu.make_async_copy(ask_ref, q_ref, kv_sem.at[2]))
    for copy in copies:
        copy.start()
    for copy in copies:
        copy.wait()
    if not own:
        keep = pltpu.make_async_copy(kv, kept_ref, kv_sem.at[3])
        keep.start()

    def step(s, slots, masked):
        keys = jnp.concatenate(
            [kv[slot, 0:half, p * features:(p + 1) * features] for slot in slots for p in (0, 1)], 0)
        values = jnp.concatenate([kv[slot, half:rows, :] for slot in slots], 1)

        def scores_of(t):
            scores = lax.dot_general(
                keys, q_ref[s, :, t * features:(t + 1) * features],
                (((1,), (1,)), ((), ())), preferred_element_type=jnp.float32,
            )
            if masked:
                scores = jnp.where(causal(scores.shape), scores, MASKED)
            return scores

        def causal(shape):
            return (lax.broadcasted_iota(jnp.int32, shape, 0)
                    <= lax.broadcasted_iota(jnp.int32, shape, 1))

        def absorb(t, scores):
            lanes = slice(t * rows, (t + 1) * rows)
            before = top[:, lanes]
            now = jnp.maximum(before, jnp.max(scores, axis=0, keepdims=True))
            top[:, lanes] = now
            weights = jnp.exp2((scores - now[0:1]) * FACTOR)
            if masked:
                weights = jnp.where(causal(scores.shape), weights, 0.0)
            shrink = jnp.exp2((before - now) * FACTOR)
            total[:, lanes] = total[:, lanes] * shrink + jnp.sum(weights, axis=0, keepdims=True)
            acc[:, lanes] = acc[:, lanes] * shrink[0:1] + jnp.dot(
                values, weights.astype(jnp.bfloat16), preferred_element_type=jnp.float32)

        scores = scores_of(0)
        for t in range(heads):
            following = scores_of(t + 1) if t + 1 < heads else None
            absorb(t, scores)
            scores = following

    @pl.loop(0, CORES if own else PEERS - CORES)
    def _(i):
        turn = lax.div(i, CORES) + (0 if own else 1)
        query_x = lax.rem(x + turn, X_SIZE)
        query_core = lax.rem(i + core, CORES)
        s = query_x * CORES + query_core
        slot = i if own else s
        query_at = place_ref[ctx_of(query_x, y, query_core)]

        def note(i, found):
            slot_core = jnp.where(i < Y_SIZE, core, 1 - core)
            key_at = place_ref[ctx_of(x, lax.rem(i, Y_SIZE), slot_core)]
            listed[found] = i
            return found + (key_at < query_at).astype(jnp.int32)

        found = lax.fori_loop(0, SLOTS, note, jnp.int32(0))
        top[...] = jnp.full_like(top, MASKED)
        total[...] = jnp.zeros_like(total)
        acc[...] = jnp.zeros_like(acc)

        if own:
            step(s, [jnp.where(query_core == core, y, Y_SIZE + y)], True)

        fours = lax.div(found, 4)

        @pl.loop(0, fours)
        def _(i):
            step(s, [listed[4 * i + j] for j in range(4)], False)

        rest = found - 4 * fours

        @pl.when(rest >= 2)
        def _():
            step(s, [listed[4 * fours], listed[4 * fours + 1]], False)

        @pl.when(lax.rem(rest, 2) == 1)
        def _():
            step(s, [listed[found - 1]], False)

        row = lax.broadcasted_iota(jnp.int32, (STAT_ROWS, rows), 0)
        stats = jnp.zeros((STAT_ROWS, rows), jnp.float32)
        for t in range(heads):
            lanes = slice(t * rows, (t + 1) * rows)
            norm = jnp.maximum(total[0:1, lanes], 1e-30)
            out_ref[slot, t * features:(t + 1) * features, :] = (
                acc[:, lanes] * (1.0 / norm)).astype(jnp.bfloat16)
            left = top[0:1, lanes] * FACTOR + jnp.log(norm) * LOG2_E
            for part in range(3):
                piece = left.astype(jnp.bfloat16).astype(jnp.float32)
                stats = jnp.where(row == 3 * t + part, piece, stats)
                left = left - piece
        out_ref[slot, heads * features:heads * features + STAT_ROWS, :] = stats.astype(jnp.bfloat16)

    if not own:
        keep.wait()


def merge_kernel(heads, groups, part_ref, own_ref, mate_ref, weight_ref, out_ref,
                 hidden, chip, weight, sems):
    features = HEAD_FEATURES
    width = 2 * features
    me = lax.axis_index("ctx")
    core = lax.rem(me, CORES)
    x = lax.div(me, CORES * Y_SIZE)
    copies = [
        pltpu.make_async_copy(weight_ref.at[j], weight.at[j], sems.at[j]) for j in range(PEERS)
    ]
    for copy in copies:
        copy.start()
    chip[core] = own_ref[0]
    chip[1 - core] = mate_ref[0]

    for c in range(CORES):
        sources = [chip.at[c]] + [
            part_ref.at[lax.rem(x + turn, X_SIZE) * CORES + c] for turn in range(1, X_SIZE)
        ]
        stats = [
            source[heads * features:heads * features + STAT_ROWS, :].astype(jnp.float32)
            for source in sources
        ]
        for t in range(heads):
            levels = [
                stat[3 * t:3 * t + 1] + stat[3 * t + 1:3 * t + 2] + stat[3 * t + 2:3 * t + 3]
                for stat in stats
            ]
            peak = functools.reduce(jnp.maximum, levels)
            shares = [jnp.exp2(level - peak) for level in levels]
            inverse = 1.0 / sum(shares)
            merged = sum(
                source[t * features:(t + 1) * features, :].astype(jnp.float32)
                * (share * inverse)
                for source, share in zip(sources, shares)
            )
            at = (c * heads + t) * features
            hidden[:, at:at + features] = merged.T.astype(jnp.bfloat16)

    lines = X_SIZE * Y_SIZE // groups
    parts = Y_SIZE // lines
    part_rows = weight.shape[2] // 2
    for g in range(groups):
        if g % parts == 0:
            for c in range(CORES):
                copies[(g // parts) * CORES + c].wait()
        term = None
        for side in range(2):
            start = (g % parts) * lines
            piece = jnp.concatenate([
                weight[(g // parts) * CORES + c, start + line,
                           side * part_rows:(side + 1) * part_rows, :]
                for line in range(lines) for c in range(CORES)
            ], 0)
            product = lax.dot_general(
                hidden[:, side * width:(side + 1) * width], piece,
                (((1,), (1,)), ((), ())), preferred_element_type=jnp.float32,
            )
            term = product if term is None else term + product
        out_ref[g] = term.astype(jnp.bfloat16)


def hold(array):
    return pl.pallas_call(
        lambda array_ref, out_ref: None,
        out_shape=jax.ShapeDtypeStruct(array.shape, array.dtype),
        in_specs=[pl.BlockSpec(memory_space=pl.ANY)],
        out_specs=pl.BlockSpec(memory_space=pl.ANY),
        input_output_aliases={0: 0},
        name="hold",
    )(array)


def body(placement, queries, keys, values, out_weight):
    rows, columns = queries.shape
    blocks = placement.shape[0]
    width = 2 * HEAD_FEATURES
    heads = columns // HEAD_FEATURES // CORES
    groups = lax.axis_size("head")

    turned = out_weight.T
    sent = pl.pallas_call(
        pack_kernel,
        out_shape=jax.ShapeDtypeStruct((rows + 2 * turned.shape[0], width), jnp.bfloat16),
        in_specs=[pl.BlockSpec(memory_space=pltpu.VMEM)] * 3,
        out_specs=pl.BlockSpec(memory_space=pltpu.VMEM),
        name="pack",
    )(keys, values, turned)
    line = lax.all_gather(sent, "ctx", axis=0, axis_index_groups=Y_GROUPS)

    asked = jnp.stack([queries[:, c * width:(c + 1) * width] for c in range(CORES)], 0)
    asked = jnp.broadcast_to(asked[None], (X_SIZE,) + asked.shape).reshape(PEERS, rows, width)
    asked = lax.all_to_all(asked, "ctx", 0, 0, tiled=True, axis_index_groups=XC_GROUPS)
    asked = hold(asked)
    asked = pltpu.with_memory_space_constraint(asked, pltpu.HBM)
    swap = [(i, i ^ 1) for i in range(blocks)]
    other = lax.ppermute(line, "ctx", swap)
    held = pltpu.with_memory_space_constraint(line, pltpu.HBM)
    spread = line[:, rows:]
    weights = lax.all_gather(spread, "ctx", axis=0, axis_index_groups=XC_GROUPS)
    weights = pltpu.with_memory_space_constraint(weights, pltpu.HBM)

    def attend(own, *lines):
        count = CORES if own else PEERS
        out_shape = [jax.ShapeDtypeStruct((count, width + STAT_ROWS, rows), jnp.bfloat16)]
        out_specs = [pl.BlockSpec(memory_space=pltpu.VMEM)]
        if not own:
            out_shape.append(jax.ShapeDtypeStruct((SLOTS, rows, width), jnp.bfloat16))
            out_specs.append(pl.BlockSpec(memory_space=pltpu.HBM))
        return pl.pallas_call(
            functools.partial(attend_kernel, own, rows, heads),
            out_shape=out_shape,
            in_specs=[
                pl.BlockSpec(memory_space=pltpu.SMEM),
                pl.BlockSpec(memory_space=pltpu.HBM),
            ] + [pl.BlockSpec(memory_space=pl.ANY)] * len(lines),
            out_specs=out_specs,
            scratch_shapes=[
                pltpu.SMEM((SLOTS + 1,), jnp.int32),
                pltpu.VMEM((PEERS, rows, width), jnp.bfloat16),
                pltpu.VMEM((SLOTS, rows, width), jnp.bfloat16),
                pltpu.VMEM((8, heads * rows), jnp.float32),
                pltpu.VMEM((8, heads * rows), jnp.float32),
                pltpu.VMEM((HEAD_FEATURES, heads * rows), jnp.float32),
                pltpu.SemaphoreType.DMA((4,)),
            ],
            compiler_params=pltpu.CompilerParams(
                vmem_limit_bytes=(32 << 20) if own else 62900000),
            cost_estimate=pl.CostEstimate(
                flops=1_000_000_000 * count, transcendentals=1_000_000 * count,
                bytes_accessed=5_000_000),
        )(placement, asked, *lines)

    parts, kept = attend(False, held, other)
    kept = pltpu.with_memory_space_constraint(kept, pltpu.HBM)
    gathered = lax.all_to_all(parts, "ctx", 0, 0, tiled=True, axis_index_groups=XC_GROUPS)
    near, = attend(True, kept)
    mate = lax.ppermute(near[1:], "ctx", swap)

    out_columns = blocks * turned.shape[0] // groups
    terms = pl.pallas_call(
        functools.partial(merge_kernel, heads, groups),
        out_shape=jax.ShapeDtypeStruct((groups, rows, out_columns), jnp.bfloat16),
        in_specs=[
            pl.BlockSpec(memory_space=pltpu.VMEM),
        ] * 3 + [pl.BlockSpec(memory_space=pltpu.HBM)],
        out_specs=pl.BlockSpec(memory_space=pltpu.VMEM),
        scratch_shapes=[
            pltpu.VMEM((rows, columns), jnp.bfloat16),
            pltpu.VMEM((CORES, width + STAT_ROWS, rows), jnp.bfloat16),
            pltpu.VMEM(weights.shape, jnp.bfloat16),
            pltpu.SemaphoreType.DMA((PEERS,)),
        ],
        compiler_params=pltpu.CompilerParams(vmem_limit_bytes=32 * 1024 * 1024),
        name="merge_project",
    )(gathered, near, mate, weights)
    return lax.psum_scatter(
        terms.reshape(groups * rows, out_columns), "head", scatter_dimension=0, tiled=True
    )


def solution(mesh):
    placed = (P(), P("ctx", "head"), P("ctx", "head"), P("ctx", "head"), P("head", "ctx"))

    return jax.shard_map(
        body, mesh=mesh, in_specs=placed, out_specs=P("ctx", "head"), check_vma=False
    )
```

```python
import functools

import jax
import jax.numpy as jnp
from jax import lax
from jax.experimental import pallas as pl
from jax.experimental.pallas import tpu as pltpu
from jax.sharding import PartitionSpec as P

HEAD_FEATURES = 128
MASKED = -1e30
LOG2_E = 1.4426950408889634
FACTOR = HEAD_FEATURES ** (-0.5) * LOG2_E
X_SIZE, Y_SIZE, CORES = 4, 8, 2
PEERS = X_SIZE * CORES
SLOTS = Y_SIZE * CORES
STAT_ROWS = 16


def ctx_of(x, y, core):
    return (x * Y_SIZE + y) * CORES + core


X_GROUPS = [[ctx_of(x, y, c) for x in range(X_SIZE)] for y in range(Y_SIZE) for c in range(CORES)]
Y_GROUPS = [[ctx_of(x, y, c) for y in range(Y_SIZE)] for x in range(X_SIZE) for c in range(CORES)]
XC_GROUPS = [[ctx_of(x, y, c) for x in range(X_SIZE) for c in range(CORES)] for y in range(Y_SIZE)]


def pack_kernel(key_ref, value_ref, out_ref):
    rows, features = key_ref.shape
    half = rows // 2
    width = out_ref.shape[1]
    out_ref[0:half, 0:features] = key_ref[0:half, :]
    out_ref[0:half, features:width] = key_ref[half:rows, :]
    out_ref[half:rows, :] = value_ref[...].astype(jnp.float32).T.astype(jnp.bfloat16)


def attend_kernel(own, rows, heads, place_ref, ask_ref, *refs):
    features = HEAD_FEATURES
    half = rows // 2
    me = lax.axis_index("ctx")
    core = lax.rem(me, CORES)
    y = lax.rem(lax.div(me, CORES), Y_SIZE)
    x = lax.div(me, CORES * Y_SIZE)

    if own:
        kept_ref, out_ref, listed, q_ref, kv, top, total, acc, kv_sem = refs
        copies = [pltpu.make_async_copy(kept_ref, kv, kv_sem.at[0])]
    else:
        line_ref, other_ref, out_ref, kept_ref, listed, q_ref, kv, top, total, acc, kv_sem = refs
        copies = [
            pltpu.make_async_copy(
                line_ref, kv.at[pl.ds(0, Y_SIZE)], kv_sem.at[0]),
            pltpu.make_async_copy(
                other_ref, kv.at[pl.ds(Y_SIZE, Y_SIZE)], kv_sem.at[1]),
        ]
    copies.append(pltpu.make_async_copy(ask_ref, q_ref, kv_sem.at[2]))
    for copy in copies:
        copy.start()
    for copy in copies:
        copy.wait()
    if not own:
        keep = pltpu.make_async_copy(kv, kept_ref, kv_sem.at[3])
        keep.start()

    def step(s, slots, masked):
        keys = jnp.concatenate(
            [kv[slot, 0:half, p * features:(p + 1) * features] for slot in slots for p in (0, 1)], 0)
        values = jnp.concatenate([kv[slot, half:rows, :] for slot in slots], 1)

        def scores_of(t):
            scores = lax.dot_general(
                keys, q_ref[s, :, t * features:(t + 1) * features],
                (((1,), (1,)), ((), ())), preferred_element_type=jnp.float32,
            )
            if masked:
                scores = jnp.where(causal(scores.shape), scores, MASKED)
            return scores

        def causal(shape):
            return (lax.broadcasted_iota(jnp.int32, shape, 0)
                    <= lax.broadcasted_iota(jnp.int32, shape, 1))

        def absorb(t, scores):
            lanes = slice(t * rows, (t + 1) * rows)
            before = top[:, lanes]
            now = jnp.maximum(before, jnp.max(scores, axis=0, keepdims=True))
            top[:, lanes] = now
            weights = jnp.exp2((scores - now[0:1]) * FACTOR)
            if masked:
                weights = jnp.where(causal(scores.shape), weights, 0.0)
            shrink = jnp.exp2((before - now) * FACTOR)
            total[:, lanes] = total[:, lanes] * shrink + jnp.sum(weights, axis=0, keepdims=True)
            acc[:, lanes] = acc[:, lanes] * shrink[0:1] + jnp.dot(
                values, weights.astype(jnp.bfloat16), preferred_element_type=jnp.float32)

        scores = scores_of(0)
        for t in range(heads):
            following = scores_of(t + 1) if t + 1 < heads else None
            absorb(t, scores)
            scores = following

    @pl.loop(0, CORES if own else PEERS - CORES)
    def _(i):
        turn = lax.div(i, CORES) + (0 if own else 1)
        query_x = lax.rem(x + turn, X_SIZE)
        query_core = lax.rem(i + core, CORES)
        s = query_x * CORES + query_core
        slot = i if own else s
        query_at = place_ref[ctx_of(query_x, y, query_core)]

        found = jnp.int32(0)
        for i in range(SLOTS):
            slot_core = core if i < Y_SIZE else 1 - core
            key_at = place_ref[ctx_of(x, i % Y_SIZE, slot_core)]
            listed[found] = jnp.int32(i)
            found = found + (key_at < query_at).astype(jnp.int32)
        top[...] = jnp.full_like(top, MASKED)
        total[...] = jnp.zeros_like(total)
        acc[...] = jnp.zeros_like(acc)

        if own:
            step(s, [jnp.where(query_core == core, y, Y_SIZE + y)], True)

        fours = lax.div(found, 4)

        @pl.loop(0, fours)
        def _(i):
            step(s, [listed[4 * i + j] for j in range(4)], False)

        rest = found - 4 * fours

        @pl.when(rest >= 2)
        def _():
            step(s, [listed[4 * fours], listed[4 * fours + 1]], False)

        @pl.when(lax.rem(rest, 2) == 1)
        def _():
            step(s, [listed[found - 1]], False)

        row = lax.broadcasted_iota(jnp.int32, (STAT_ROWS, rows), 0)
        stats = jnp.zeros((STAT_ROWS, rows), jnp.float32)
        for t in range(heads):
            lanes = slice(t * rows, (t + 1) * rows)
            norm = jnp.maximum(total[0:1, lanes], 1e-30)
            out_ref[slot, t * features:(t + 1) * features, :] = (
                acc[:, lanes] * (1.0 / norm)).astype(jnp.bfloat16)
            left = top[0:1, lanes] * FACTOR + jnp.log(norm) * LOG2_E
            for part in range(3):
                piece = left.astype(jnp.bfloat16).astype(jnp.float32)
                stats = jnp.where(row == 3 * t + part, piece, stats)
                left = left - piece
        out_ref[slot, heads * features:heads * features + STAT_ROWS, :] = stats.astype(jnp.bfloat16)

    if not own:
        keep.wait()


def merge_kernel(heads, groups, part_ref, own_ref, mate_ref, weight_ref, mirror_ref, out_ref,
                 hidden, chip, weight, sems):
    features = HEAD_FEATURES
    width = 2 * features
    me = lax.axis_index("ctx")
    core = lax.rem(me, CORES)
    x = lax.div(me, CORES * Y_SIZE)
    copies = [
        pltpu.make_async_copy(
            source.at[:, i], weight.at[i * CORES + side], sems.at[2 * i + turn])
        for i in range(X_SIZE)
        for turn, (source, side) in enumerate(((weight_ref, core), (mirror_ref, 1 - core)))
    ]
    for copy in copies:
        copy.start()
    chip[core] = own_ref[0]
    chip[1 - core] = mate_ref[0]

    for c in range(CORES):
        sources = [chip.at[c]] + [
            part_ref.at[lax.rem(x + turn, X_SIZE) * CORES + c] for turn in range(1, X_SIZE)
        ]
        stats = [
            source[heads * features:heads * features + STAT_ROWS, :].astype(jnp.float32)
            for source in sources
        ]
        for t in range(heads):
            levels = [
                stat[3 * t:3 * t + 1] + stat[3 * t + 1:3 * t + 2] + stat[3 * t + 2:3 * t + 3]
                for stat in stats
            ]
            peak = functools.reduce(jnp.maximum, levels)
            shares = [jnp.exp2(level - peak) for level in levels]
            inverse = 1.0 / sum(shares)
            merged = sum(
                source[t * features:(t + 1) * features, :].astype(jnp.float32)
                * (share * inverse)
                for source, share in zip(sources, shares)
            )
            at = (c * heads + t) * features
            hidden[:, at:at + features] = merged.T.astype(jnp.bfloat16)

    lines = X_SIZE * Y_SIZE // groups
    parts = Y_SIZE // lines
    part_rows = weight.shape[2] // 2
    for g in range(groups):
        if g % parts == 0:
            for c in range(CORES):
                copies[(g // parts) * CORES + c].wait()
        term = None
        for side in range(2):
            start = (g % parts) * lines
            piece = jnp.concatenate([
                weight[(g // parts) * CORES + c, start + line,
                           side * part_rows:(side + 1) * part_rows, :]
                for line in range(lines) for c in range(CORES)
            ], 0)
            product = lax.dot_general(
                hidden[:, side * width:(side + 1) * width], piece,
                (((1,), (1,)), ((), ())), preferred_element_type=jnp.float32,
            )
            term = product if term is None else term + product
        out_ref[g] = term.astype(jnp.bfloat16)


def hold(array):
    return pl.pallas_call(
        lambda array_ref, out_ref: None,
        out_shape=jax.ShapeDtypeStruct(array.shape, array.dtype),
        in_specs=[pl.BlockSpec(memory_space=pl.ANY)],
        out_specs=pl.BlockSpec(memory_space=pl.ANY),
        input_output_aliases={0: 0},
        name="hold",
    )(array)


def body(placement, queries, keys, values, out_weight):
    rows, columns = queries.shape
    blocks = placement.shape[0]
    width = 2 * HEAD_FEATURES
    heads = columns // HEAD_FEATURES // CORES
    groups = lax.axis_size("head")

    turned = out_weight.T
    sent = pl.pallas_call(
        pack_kernel,
        out_shape=jax.ShapeDtypeStruct((rows, width), jnp.bfloat16),
        in_specs=[pl.BlockSpec(memory_space=pltpu.VMEM)] * 2,
        out_specs=pl.BlockSpec(memory_space=pltpu.VMEM),
        name="pack",
    )(keys, values)
    line = lax.all_gather(sent, "ctx", axis=0, axis_index_groups=Y_GROUPS)

    asked = jnp.stack([queries[:, c * width:(c + 1) * width] for c in range(CORES)], 0)
    asked = jnp.broadcast_to(asked[None], (X_SIZE,) + asked.shape).reshape(PEERS, rows, width)
    asked = lax.all_to_all(asked, "ctx", 0, 0, tiled=True, axis_index_groups=XC_GROUPS)
    asked = hold(asked)
    asked = pltpu.with_memory_space_constraint(asked, pltpu.HBM)
    column = jnp.concatenate([turned[:, :width], turned[:, width:]], 0)
    column = jnp.broadcast_to(column[None], (X_SIZE,) + column.shape)
    column = lax.all_to_all(column, "ctx", 0, 0, tiled=True, axis_index_groups=X_GROUPS)
    column = hold(column)
    swap = [(i, i ^ 1) for i in range(blocks)]
    other = lax.ppermute(line, "ctx", swap)
    held = pltpu.with_memory_space_constraint(line, pltpu.HBM)
    weights = lax.all_gather(column, "ctx", axis=0, axis_index_groups=Y_GROUPS)
    weights = pltpu.with_memory_space_constraint(weights, pltpu.HBM)
    mirrored = lax.ppermute(weights, "ctx", swap)
    mirrored = pltpu.with_memory_space_constraint(mirrored, pltpu.HBM)

    def attend(own, *lines):
        count = CORES if own else PEERS
        out_shape = [jax.ShapeDtypeStruct((count, width + STAT_ROWS, rows), jnp.bfloat16)]
        out_specs = [pl.BlockSpec(memory_space=pltpu.VMEM)]
        if not own:
            out_shape.append(jax.ShapeDtypeStruct((SLOTS, rows, width), jnp.bfloat16))
            out_specs.append(pl.BlockSpec(memory_space=pltpu.HBM))
        return pl.pallas_call(
            functools.partial(attend_kernel, own, rows, heads),
            out_shape=out_shape,
            in_specs=[
                pl.BlockSpec(memory_space=pltpu.SMEM),
                pl.BlockSpec(memory_space=pltpu.HBM),
            ] + [pl.BlockSpec(memory_space=pl.ANY)] * len(lines),
            out_specs=out_specs,
            scratch_shapes=[
                pltpu.SMEM((SLOTS + 1,), jnp.int32),
                pltpu.VMEM((PEERS, rows, width), jnp.bfloat16),
                pltpu.VMEM((SLOTS, rows, width), jnp.bfloat16),
                pltpu.VMEM((8, heads * rows), jnp.float32),
                pltpu.VMEM((8, heads * rows), jnp.float32),
                pltpu.VMEM((HEAD_FEATURES, heads * rows), jnp.float32),
                pltpu.SemaphoreType.DMA((4,)),
            ],
            compiler_params=pltpu.CompilerParams(
                vmem_limit_bytes=(32 << 20) if own else 62900000),
            cost_estimate=pl.CostEstimate(
                flops=1_000_000_000 * count, transcendentals=1_000_000 * count,
                bytes_accessed=5_000_000),
        )(placement, asked, *lines)

    parts, kept = attend(False, held, other)
    kept = pltpu.with_memory_space_constraint(kept, pltpu.HBM)
    gathered = lax.all_to_all(parts, "ctx", 0, 0, tiled=True, axis_index_groups=XC_GROUPS)
    near, = attend(True, kept)
    mate = lax.ppermute(near[1:], "ctx", swap)

    out_columns = blocks * turned.shape[0] // groups
    terms = pl.pallas_call(
        functools.partial(merge_kernel, heads, groups),
        out_shape=jax.ShapeDtypeStruct((groups, rows, out_columns), jnp.bfloat16),
        in_specs=[
            pl.BlockSpec(memory_space=pltpu.VMEM),
        ] * 3 + [pl.BlockSpec(memory_space=pltpu.HBM)] * 2,
        out_specs=pl.BlockSpec(memory_space=pltpu.VMEM),
        scratch_shapes=[
            pltpu.VMEM((rows, columns), jnp.bfloat16),
            pltpu.VMEM((CORES, width + STAT_ROWS, rows), jnp.bfloat16),
            pltpu.VMEM((PEERS, Y_SIZE) + weights.shape[-2:], jnp.bfloat16),
            pltpu.SemaphoreType.DMA((PEERS,)),
        ],
        compiler_params=pltpu.CompilerParams(vmem_limit_bytes=32 * 1024 * 1024),
        name="merge_project",
    )(gathered, near, mate, weights, mirrored)
    return lax.psum_scatter(
        terms.reshape(groups * rows, out_columns), "head", scatter_dimension=0, tiled=True
    )


def solution(mesh):
    placed = (P(), P("ctx", "head"), P("ctx", "head"), P("ctx", "head"), P("head", "ctx"))

    return jax.shard_map(
        body, mesh=mesh, in_specs=placed, out_specs=P("ctx", "head"), check_vma=False
    )
```

```python
import functools

import jax
import jax.numpy as jnp
from jax import lax
from jax.experimental import pallas as pl
from jax.experimental.pallas import tpu as pltpu
from jax.sharding import PartitionSpec as P

HEAD_FEATURES = 128
MASKED = -1e30
LOG2_E = 1.4426950408889634
FACTOR = HEAD_FEATURES ** (-0.5) * LOG2_E
X_SIZE, Y_SIZE, CORES = 4, 8, 2
PEERS = X_SIZE * CORES
SLOTS = Y_SIZE * CORES
STAT_ROWS = 16


def ctx_of(x, y, core):
    return (x * Y_SIZE + y) * CORES + core


X_GROUPS = [[ctx_of(x, y, c) for x in range(X_SIZE)] for y in range(Y_SIZE) for c in range(CORES)]
Y_GROUPS = [[ctx_of(x, y, c) for y in range(Y_SIZE)] for x in range(X_SIZE) for c in range(CORES)]
XC_GROUPS = [[ctx_of(x, y, c) for x in range(X_SIZE) for c in range(CORES)] for y in range(Y_SIZE)]


def pack_kernel(key_ref, value_ref, weight_ref, out_ref):
    rows, features = key_ref.shape
    half = rows // 2
    count = weight_ref.shape[0]
    width = out_ref.shape[1]
    out_ref[0:half, 0:features] = key_ref[0:half, :]
    out_ref[0:half, features:width] = key_ref[half:rows, :]
    out_ref[half:rows, :] = value_ref[...].astype(jnp.float32).T.astype(jnp.bfloat16)
    for i in range(2):
        out_ref[rows + i * count:rows + (i + 1) * count, :] = (
            weight_ref[:, i * width:(i + 1) * width])


def attend_kernel(own, rows, heads, place_ref, ask_ref, *refs):
    features = HEAD_FEATURES
    half = rows // 2
    me = lax.axis_index("ctx")
    core = lax.rem(me, CORES)
    y = lax.rem(lax.div(me, CORES), Y_SIZE)
    x = lax.div(me, CORES * Y_SIZE)

    if own:
        kept_ref, out_ref, listed, q_ref, kv, top, total, acc, kv_sem = refs
        copies = [pltpu.make_async_copy(kept_ref, kv, kv_sem.at[0])]
    else:
        line_ref, other_ref, out_ref, kept_ref, listed, q_ref, kv, top, total, acc, kv_sem = refs
        copies = [
            pltpu.make_async_copy(
                line_ref.at[:, pl.ds(0, rows), :], kv.at[pl.ds(0, Y_SIZE)], kv_sem.at[0]),
            pltpu.make_async_copy(
                other_ref.at[:, pl.ds(0, rows), :], kv.at[pl.ds(Y_SIZE, Y_SIZE)], kv_sem.at[1]),
        ]
    copies.append(pltpu.make_async_copy(ask_ref, q_ref, kv_sem.at[2]))
    for copy in copies:
        copy.start()
    for copy in copies:
        copy.wait()
    if not own:
        keep = pltpu.make_async_copy(kv, kept_ref, kv_sem.at[3])
        keep.start()

    def step(s, slots, masked):
        keys = jnp.concatenate(
            [kv[slot, 0:half, p * features:(p + 1) * features] for slot in slots for p in (0, 1)], 0)
        values = jnp.concatenate([kv[slot, half:rows, :] for slot in slots], 1)

        def scores_of(t):
            scores = lax.dot_general(
                keys, q_ref[s, :, t * features:(t + 1) * features],
                (((1,), (1,)), ((), ())), preferred_element_type=jnp.float32,
            )
            if masked:
                scores = jnp.where(causal(scores.shape), scores, MASKED)
            return scores

        def causal(shape):
            return (lax.broadcasted_iota(jnp.int32, shape, 0)
                    <= lax.broadcasted_iota(jnp.int32, shape, 1))

        def absorb(t, scores):
            lanes = slice(t * rows, (t + 1) * rows)
            before = top[:, lanes]
            now = jnp.maximum(before, jnp.max(scores, axis=0, keepdims=True))
            top[:, lanes] = now
            weights = jnp.exp2((scores - now[0:1]) * FACTOR)
            if masked:
                weights = jnp.where(causal(scores.shape), weights, 0.0)
            shrink = jnp.exp2((before - now) * FACTOR)
            total[:, lanes] = total[:, lanes] * shrink + jnp.sum(weights, axis=0, keepdims=True)
            acc[:, lanes] = acc[:, lanes] * shrink[0:1] + jnp.dot(
                values, weights.astype(jnp.bfloat16), preferred_element_type=jnp.float32)

        scores = scores_of(0)
        for t in range(heads):
            following = scores_of(t + 1) if t + 1 < heads else None
            absorb(t, scores)
            scores = following

    @pl.loop(0, CORES if own else PEERS - CORES)
    def _(i):
        turn = lax.div(i, CORES) + (0 if own else 1)
        query_x = lax.rem(x + turn, X_SIZE)
        query_core = lax.rem(i + core, CORES)
        s = query_x * CORES + query_core
        slot = i if own else s
        query_at = place_ref[ctx_of(query_x, y, query_core)]

        found = jnp.int32(0)
        for i in range(SLOTS):
            slot_core = core if i < Y_SIZE else 1 - core
            key_at = place_ref[ctx_of(x, i % Y_SIZE, slot_core)]
            listed[found] = jnp.int32(i)
            found = found + (key_at < query_at).astype(jnp.int32)
        top[...] = jnp.full_like(top, MASKED)
        total[...] = jnp.zeros_like(total)
        acc[...] = jnp.zeros_like(acc)

        if own:
            step(s, [jnp.where(query_core == core, y, Y_SIZE + y)], True)

        fours = lax.div(found, 4)

        @pl.loop(0, fours)
        def _(i):
            step(s, [listed[4 * i + j] for j in range(4)], False)

        rest = found - 4 * fours

        @pl.when(rest >= 2)
        def _():
            step(s, [listed[4 * fours], listed[4 * fours + 1]], False)

        @pl.when(lax.rem(rest, 2) == 1)
        def _():
            step(s, [listed[found - 1]], False)

        row = lax.broadcasted_iota(jnp.int32, (STAT_ROWS, rows), 0)
        stats = jnp.zeros((STAT_ROWS, rows), jnp.float32)
        for t in range(heads):
            lanes = slice(t * rows, (t + 1) * rows)
            norm = jnp.maximum(total[0:1, lanes], 1e-30)
            out_ref[slot, t * features:(t + 1) * features, :] = (
                acc[:, lanes] * (1.0 / norm)).astype(jnp.bfloat16)
            left = top[0:1, lanes] * FACTOR + jnp.log(norm) * LOG2_E
            for part in range(3):
                piece = left.astype(jnp.bfloat16).astype(jnp.float32)
                stats = jnp.where(row == 3 * t + part, piece, stats)
                left = left - piece
        out_ref[slot, heads * features:heads * features + STAT_ROWS, :] = stats.astype(jnp.bfloat16)

    if not own:
        keep.wait()


def merge_kernel(rows, heads, groups, part_ref, own_ref, mate_ref, line_ref, other_ref,
                 weight_ref, mirror_ref, out_ref,
                 hidden, chip, weight, sems):
    features = HEAD_FEATURES
    width = 2 * features
    me = lax.axis_index("ctx")
    core = lax.rem(me, CORES)
    x = lax.div(me, CORES * Y_SIZE)
    count = weight.shape[3]
    copies = [
        pltpu.make_async_copy(
            line_ref.at[:, pl.ds(rows, count), :], weight.at[0, core], sems.at[0]),
        pltpu.make_async_copy(
            other_ref.at[:, pl.ds(rows, count), :], weight.at[0, 1 - core], sems.at[1]),
    ]
    for i in range(1, X_SIZE):
        for turned, (source, side) in enumerate(((weight_ref, core), (mirror_ref, 1 - core))):
            copies.append(pltpu.make_async_copy(
                source.at[:, i - 1], weight.at[i, side], sems.at[2 * i + turned]))
    for copy in copies:
        copy.start()
    chip[core] = own_ref[0]
    chip[1 - core] = mate_ref[0]

    for c in range(CORES):
        sources = [chip.at[c]] + [
            part_ref.at[lax.rem(x + turn, X_SIZE) * CORES + c] for turn in range(1, X_SIZE)
        ]
        stats = [
            source[heads * features:heads * features + STAT_ROWS, :].astype(jnp.float32)
            for source in sources
        ]
        for t in range(heads):
            levels = [
                stat[3 * t:3 * t + 1] + stat[3 * t + 1:3 * t + 2] + stat[3 * t + 2:3 * t + 3]
                for stat in stats
            ]
            peak = functools.reduce(jnp.maximum, levels)
            shares = [jnp.exp2(level - peak) for level in levels]
            inverse = 1.0 / sum(shares)
            merged = sum(
                source[t * features:(t + 1) * features, :].astype(jnp.float32)
                * (share * inverse)
                for source, share in zip(sources, shares)
            )
            at = (c * heads + t) * features
            hidden[:, at:at + features] = merged.T.astype(jnp.bfloat16)

    lines = X_SIZE * Y_SIZE // groups
    parts = Y_SIZE // lines
    part_rows = count // 2
    for i in range(X_SIZE):
        for copy in copies[2 * i:2 * i + 2]:
            copy.wait()
        for p in range(parts):
            term = None
            for side in range(2):
                piece = jnp.concatenate([
                    weight[i, c, p * lines + line, side * part_rows:(side + 1) * part_rows, :]
                    for line in range(lines) for c in range(CORES)
                ], 0)
                product = lax.dot_general(
                    hidden[:, side * width:(side + 1) * width], piece,
                    (((1,), (1,)), ((), ())), preferred_element_type=jnp.float32,
                )
                term = product if term is None else term + product
            out_ref[lax.rem(x + i, X_SIZE) * parts + p] = term.astype(jnp.bfloat16)


def hold(array):
    return pl.pallas_call(
        lambda array_ref, out_ref: None,
        out_shape=jax.ShapeDtypeStruct(array.shape, array.dtype),
        in_specs=[pl.BlockSpec(memory_space=pl.ANY)],
        out_specs=pl.BlockSpec(memory_space=pl.ANY),
        input_output_aliases={0: 0},
        name="hold",
    )(array)


def turn_kernel(column_ref, out_ref):
    x = lax.div(lax.axis_index("ctx"), CORES * Y_SIZE)
    for i in range(X_SIZE - 1):
        out_ref[i] = column_ref[lax.rem(x + 1 + i, X_SIZE)]


def turn(column):
    return pl.pallas_call(
        turn_kernel,
        out_shape=jax.ShapeDtypeStruct((X_SIZE - 1,) + column.shape[1:], column.dtype),
        in_specs=[pl.BlockSpec(memory_space=pltpu.VMEM)],
        out_specs=pl.BlockSpec(memory_space=pltpu.VMEM),
        name="turn",
    )(column)


def body(placement, queries, keys, values, out_weight):
    rows, columns = queries.shape
    blocks = placement.shape[0]
    width = 2 * HEAD_FEATURES
    heads = columns // HEAD_FEATURES // CORES
    groups = lax.axis_size("head")

    turned = out_weight.T
    sent = pl.pallas_call(
        pack_kernel,
        out_shape=jax.ShapeDtypeStruct((rows + 2 * turned.shape[0], width), jnp.bfloat16),
        in_specs=[pl.BlockSpec(memory_space=pltpu.VMEM)] * 3,
        out_specs=pl.BlockSpec(memory_space=pltpu.VMEM),
        name="pack",
    )(keys, values, turned)
    line = lax.all_gather(sent, "ctx", axis=0, axis_index_groups=Y_GROUPS)

    asked = jnp.stack([queries[:, c * width:(c + 1) * width] for c in range(CORES)], 0)
    asked = jnp.broadcast_to(asked[None], (X_SIZE,) + asked.shape).reshape(PEERS, rows, width)
    asked = lax.all_to_all(asked, "ctx", 0, 0, tiled=True, axis_index_groups=XC_GROUPS)
    asked = hold(asked)
    asked = pltpu.with_memory_space_constraint(asked, pltpu.HBM)
    column = jnp.concatenate([turned[:, :width], turned[:, width:]], 0)
    column = jnp.broadcast_to(column[None], (X_SIZE,) + column.shape)
    column = lax.all_to_all(column, "ctx", 0, 0, tiled=True, axis_index_groups=X_GROUPS)
    column = turn(column)
    swap = [(i, i ^ 1) for i in range(blocks)]
    other = lax.ppermute(line, "ctx", swap)
    held = pltpu.with_memory_space_constraint(line, pltpu.HBM)
    weights = lax.all_gather(column, "ctx", axis=0, axis_index_groups=Y_GROUPS)
    weights = pltpu.with_memory_space_constraint(weights, pltpu.HBM)
    mirrored = lax.ppermute(weights, "ctx", swap)
    mirrored = pltpu.with_memory_space_constraint(mirrored, pltpu.HBM)

    def attend(own, *lines):
        count = CORES if own else PEERS
        out_shape = [jax.ShapeDtypeStruct((count, width + STAT_ROWS, rows), jnp.bfloat16)]
        out_specs = [pl.BlockSpec(memory_space=pltpu.VMEM)]
        if not own:
            out_shape.append(jax.ShapeDtypeStruct((SLOTS, rows, width), jnp.bfloat16))
            out_specs.append(pl.BlockSpec(memory_space=pltpu.HBM))
        return pl.pallas_call(
            functools.partial(attend_kernel, own, rows, heads),
            out_shape=out_shape,
            in_specs=[
                pl.BlockSpec(memory_space=pltpu.SMEM),
                pl.BlockSpec(memory_space=pltpu.HBM),
            ] + [pl.BlockSpec(memory_space=pl.ANY)] * len(lines),
            out_specs=out_specs,
            scratch_shapes=[
                pltpu.SMEM((SLOTS + 1,), jnp.int32),
                pltpu.VMEM((PEERS, rows, width), jnp.bfloat16),
                pltpu.VMEM((SLOTS, rows, width), jnp.bfloat16),
                pltpu.VMEM((8, heads * rows), jnp.float32),
                pltpu.VMEM((8, heads * rows), jnp.float32),
                pltpu.VMEM((HEAD_FEATURES, heads * rows), jnp.float32),
                pltpu.SemaphoreType.DMA((4,)),
            ],
            compiler_params=pltpu.CompilerParams(
                vmem_limit_bytes=(32 << 20) if own else 62900000),
            cost_estimate=pl.CostEstimate(
                flops=1_000_000_000 * count, transcendentals=1_000_000 * count,
                bytes_accessed=5_000_000),
        )(placement, asked, *lines)

    parts, kept = attend(False, held, other)
    kept = pltpu.with_memory_space_constraint(kept, pltpu.HBM)
    gathered = lax.all_to_all(parts, "ctx", 0, 0, tiled=True, axis_index_groups=XC_GROUPS)
    near, = attend(True, kept)
    mate = hold(lax.ppermute(near[1:], "ctx", swap))

    out_columns = blocks * turned.shape[0] // groups
    terms = pl.pallas_call(
        functools.partial(merge_kernel, rows, heads, groups),
        out_shape=jax.ShapeDtypeStruct((groups, rows, out_columns), jnp.bfloat16),
        in_specs=[
            pl.BlockSpec(memory_space=pltpu.VMEM),
        ] * 3 + [pl.BlockSpec(memory_space=pltpu.HBM)] * 4,
        out_specs=pl.BlockSpec(memory_space=pltpu.VMEM),
        scratch_shapes=[
            pltpu.VMEM((rows, columns), jnp.bfloat16),
            pltpu.VMEM((CORES, width + STAT_ROWS, rows), jnp.bfloat16),
            pltpu.VMEM((X_SIZE, CORES, Y_SIZE) + weights.shape[-2:], jnp.bfloat16),
            pltpu.SemaphoreType.DMA((PEERS,)),
        ],
        compiler_params=pltpu.CompilerParams(vmem_limit_bytes=32 * 1024 * 1024),
        name="merge_project",
    )(gathered, near, mate, held, other, weights, mirrored)
    return lax.psum_scatter(
        terms.reshape(groups * rows, out_columns), "head", scatter_dimension=0, tiled=True
    )


def solution(mesh):
    placed = (P(), P("ctx", "head"), P("ctx", "head"), P("ctx", "head"), P("head", "ctx"))

    return jax.shard_map(
        body, mesh=mesh, in_specs=placed, out_specs=P("ctx", "head"), check_vma=False
    )
```

```python
import functools

import jax
import jax.numpy as jnp
from jax import lax
from jax.experimental import pallas as pl
from jax.experimental.pallas import tpu as pltpu
from jax.sharding import PartitionSpec as P

HEAD_FEATURES = 128
MASKED = -1e30
LOG2_E = 1.4426950408889634
FACTOR = HEAD_FEATURES ** (-0.5) * LOG2_E
X_SIZE, Y_SIZE, CORES = 4, 8, 2
PEERS = X_SIZE * CORES
SLOTS = Y_SIZE * CORES
STAT_ROWS = 16


def ctx_of(x, y, core):
    return (x * Y_SIZE + y) * CORES + core


X_GROUPS = [[ctx_of(x, y, c) for x in range(X_SIZE)] for y in range(Y_SIZE) for c in range(CORES)]
Y_GROUPS = [[ctx_of(x, y, c) for y in range(Y_SIZE)] for x in range(X_SIZE) for c in range(CORES)]
XC_GROUPS = [[ctx_of(x, y, c) for x in range(X_SIZE) for c in range(CORES)] for y in range(Y_SIZE)]


def pack_kernel(key_ref, value_ref, weight_ref, out_ref):
    rows, features = key_ref.shape
    half = rows // 2
    count = weight_ref.shape[0]
    width = out_ref.shape[1]
    out_ref[0:half, 0:features] = key_ref[0:half, :]
    out_ref[0:half, features:width] = key_ref[half:rows, :]
    out_ref[half:rows, :] = value_ref[...].astype(jnp.float32).T.astype(jnp.bfloat16)
    for i in range(2):
        out_ref[rows + i * count:rows + (i + 1) * count, :] = (
            weight_ref[:, i * width:(i + 1) * width])


def attend_kernel(own, rows, heads, place_ref, ask_ref, *refs):
    features = HEAD_FEATURES
    half = rows // 2
    me = lax.axis_index("ctx")
    core = lax.rem(me, CORES)
    y = lax.rem(lax.div(me, CORES), Y_SIZE)
    x = lax.div(me, CORES * Y_SIZE)

    if own:
        kept_ref, out_ref, listed, q_ref, kv, top, total, acc, kv_sem = refs
        copies = [pltpu.make_async_copy(kept_ref, kv, kv_sem.at[0])]
    else:
        line_ref, other_ref, out_ref, kept_ref, listed, q_ref, kv, top, total, acc, kv_sem = refs
        copies = [
            pltpu.make_async_copy(
                line_ref.at[:, pl.ds(0, rows), :], kv.at[pl.ds(0, Y_SIZE)], kv_sem.at[0]),
            pltpu.make_async_copy(
                other_ref.at[:, pl.ds(0, rows), :], kv.at[pl.ds(Y_SIZE, Y_SIZE)], kv_sem.at[1]),
        ]
    copies.append(pltpu.make_async_copy(ask_ref, q_ref, kv_sem.at[2]))
    for copy in copies:
        copy.start()
    for copy in copies:
        copy.wait()
    if not own:
        keep = pltpu.make_async_copy(kv, kept_ref, kv_sem.at[3])
        keep.start()

    def step(s, slots, masked):
        keys = jnp.concatenate(
            [kv[slot, 0:half, p * features:(p + 1) * features] for slot in slots for p in (0, 1)], 0)
        values = jnp.concatenate([kv[slot, half:rows, :] for slot in slots], 1)

        def scores_of(t):
            scores = lax.dot_general(
                keys, q_ref[s, :, t * features:(t + 1) * features],
                (((1,), (1,)), ((), ())), preferred_element_type=jnp.float32,
            )
            if masked:
                scores = jnp.where(causal(scores.shape), scores, MASKED)
            return scores

        def causal(shape):
            return (lax.broadcasted_iota(jnp.int32, shape, 0)
                    <= lax.broadcasted_iota(jnp.int32, shape, 1))

        def absorb(t, scores):
            lanes = slice(t * rows, (t + 1) * rows)
            before = top[:, lanes]
            now = jnp.maximum(before, jnp.max(scores, axis=0, keepdims=True))
            top[:, lanes] = now
            weights = jnp.exp2((scores - now[0:1]) * FACTOR)
            if masked:
                weights = jnp.where(causal(scores.shape), weights, 0.0)
            shrink = jnp.exp2((before - now) * FACTOR)
            total[:, lanes] = total[:, lanes] * shrink + jnp.sum(weights, axis=0, keepdims=True)
            acc[:, lanes] = acc[:, lanes] * shrink[0:1] + jnp.dot(
                values, weights.astype(jnp.bfloat16), preferred_element_type=jnp.float32)

        scores = scores_of(0)
        for t in range(heads):
            following = scores_of(t + 1) if t + 1 < heads else None
            absorb(t, scores)
            scores = following

    @pl.loop(0, CORES if own else PEERS - CORES)
    def _(i):
        turn = lax.div(i, CORES) + (0 if own else 1)
        query_x = lax.rem(x + turn, X_SIZE)
        query_core = lax.rem(i + core, CORES)
        s = query_x * CORES + query_core
        slot = i if own else s
        query_at = place_ref[ctx_of(query_x, y, query_core)]

        found = jnp.int32(0)
        for i in range(SLOTS):
            slot_core = core if i < Y_SIZE else 1 - core
            key_at = place_ref[ctx_of(x, i % Y_SIZE, slot_core)]
            listed[found] = jnp.int32(i)
            found = found + (key_at < query_at).astype(jnp.int32)
        top[...] = jnp.full_like(top, MASKED)
        total[...] = jnp.zeros_like(total)
        acc[...] = jnp.zeros_like(acc)

        if own:
            step(s, [jnp.where(query_core == core, y, Y_SIZE + y)], True)

        fours = lax.div(found, 4)

        @pl.loop(0, fours)
        def _(i):
            step(s, [listed[4 * i + j] for j in range(4)], False)

        rest = found - 4 * fours

        @pl.when(rest >= 2)
        def _():
            step(s, [listed[4 * fours], listed[4 * fours + 1]], False)

        @pl.when(lax.rem(rest, 2) == 1)
        def _():
            step(s, [listed[found - 1]], False)

        row = lax.broadcasted_iota(jnp.int32, (STAT_ROWS, rows), 0)
        stats = jnp.zeros((STAT_ROWS, rows), jnp.float32)
        for t in range(heads):
            lanes = slice(t * rows, (t + 1) * rows)
            norm = jnp.maximum(total[0:1, lanes], 1e-30)
            out_ref[slot, t * features:(t + 1) * features, :] = (
                acc[:, lanes] * (1.0 / norm)).astype(jnp.bfloat16)
            left = top[0:1, lanes] * FACTOR + jnp.log(norm) * LOG2_E
            for part in range(3):
                piece = left.astype(jnp.bfloat16).astype(jnp.float32)
                stats = jnp.where(row == 3 * t + part, piece, stats)
                left = left - piece
        out_ref[slot, heads * features:heads * features + STAT_ROWS, :] = stats.astype(jnp.bfloat16)

    if not own:
        keep.wait()


def merge_kernel(rows, heads, groups, part_ref, own_ref, mate_ref, line_ref, other_ref,
                 weight_ref, mirror_ref, out_ref,
                 hidden, chip, weight, sems, near_sems):
    features = HEAD_FEATURES
    width = 2 * features
    me = lax.axis_index("ctx")
    core = lax.rem(me, CORES)
    x = lax.div(me, CORES * Y_SIZE)
    count = weight.shape[3]
    copies = [
        pltpu.make_async_copy(
            line_ref.at[:, pl.ds(rows, count), :], weight.at[0, core], sems.at[0]),
        pltpu.make_async_copy(
            other_ref.at[:, pl.ds(rows, count), :], weight.at[0, 1 - core], sems.at[1]),
    ]
    for i in range(1, X_SIZE):
        for turned, (source, side) in enumerate(((weight_ref, core), (mirror_ref, 1 - core))):
            copies.append(pltpu.make_async_copy(
                source.at[:, i - 1], weight.at[i, side], sems.at[2 * i + turned]))
    near_copies = [
        pltpu.make_async_copy(own_ref.at[0], chip.at[core], near_sems.at[0]),
        pltpu.make_async_copy(mate_ref.at[0], chip.at[1 - core], near_sems.at[1]),
    ]
    for copy in near_copies:
        copy.start()
    for copy in copies:
        copy.start()
    for copy in near_copies:
        copy.wait()

    for c in range(CORES):
        sources = [chip.at[c]] + [
            part_ref.at[lax.rem(x + turn, X_SIZE) * CORES + c] for turn in range(1, X_SIZE)
        ]
        stats = [
            source[heads * features:heads * features + STAT_ROWS, :].astype(jnp.float32)
            for source in sources
        ]
        for t in range(heads):
            levels = [
                stat[3 * t:3 * t + 1] + stat[3 * t + 1:3 * t + 2] + stat[3 * t + 2:3 * t + 3]
                for stat in stats
            ]
            peak = functools.reduce(jnp.maximum, levels)
            shares = [jnp.exp2(level - peak) for level in levels]
            inverse = 1.0 / sum(shares)
            merged = sum(
                source[t * features:(t + 1) * features, :].astype(jnp.float32)
                * (share * inverse)
                for source, share in zip(sources, shares)
            )
            at = (c * heads + t) * features
            hidden[:, at:at + features] = merged.T.astype(jnp.bfloat16)

    lines = X_SIZE * Y_SIZE // groups
    parts = Y_SIZE // lines
    part_rows = count // 2
    for i in range(X_SIZE):
        for copy in copies[2 * i:2 * i + 2]:
            copy.wait()
        for p in range(parts):
            term = None
            for side in range(2):
                piece = jnp.concatenate([
                    weight[i, c, p * lines + line, side * part_rows:(side + 1) * part_rows, :]
                    for line in range(lines) for c in range(CORES)
                ], 0)
                product = lax.dot_general(
                    hidden[:, side * width:(side + 1) * width], piece,
                    (((1,), (1,)), ((), ())), preferred_element_type=jnp.float32,
                )
                term = product if term is None else term + product
            out_ref[lax.rem(x + i, X_SIZE) * parts + p] = term.astype(jnp.bfloat16)


def hold(array):
    return pl.pallas_call(
        lambda array_ref, out_ref: None,
        out_shape=jax.ShapeDtypeStruct(array.shape, array.dtype),
        in_specs=[pl.BlockSpec(memory_space=pl.ANY)],
        out_specs=pl.BlockSpec(memory_space=pl.ANY),
        input_output_aliases={0: 0},
        name="hold",
    )(array)


def turn_kernel(column_ref, out_ref):
    x = lax.div(lax.axis_index("ctx"), CORES * Y_SIZE)
    for i in range(X_SIZE - 1):
        out_ref[i] = column_ref[lax.rem(x + 1 + i, X_SIZE)]


def turn(column):
    return pl.pallas_call(
        turn_kernel,
        out_shape=jax.ShapeDtypeStruct((X_SIZE - 1,) + column.shape[1:], column.dtype),
        in_specs=[pl.BlockSpec(memory_space=pltpu.VMEM)],
        out_specs=pl.BlockSpec(memory_space=pltpu.VMEM),
        name="turn",
    )(column)


def body(placement, queries, keys, values, out_weight):
    rows, columns = queries.shape
    blocks = placement.shape[0]
    width = 2 * HEAD_FEATURES
    heads = columns // HEAD_FEATURES // CORES
    groups = lax.axis_size("head")

    turned = out_weight.T
    sent = pl.pallas_call(
        pack_kernel,
        out_shape=jax.ShapeDtypeStruct((rows + 2 * turned.shape[0], width), jnp.bfloat16),
        in_specs=[pl.BlockSpec(memory_space=pltpu.VMEM)] * 3,
        out_specs=pl.BlockSpec(memory_space=pltpu.VMEM),
        name="pack",
    )(keys, values, turned)
    line = lax.all_gather(sent, "ctx", axis=0, axis_index_groups=Y_GROUPS)

    asked = jnp.stack([queries[:, c * width:(c + 1) * width] for c in range(CORES)], 0)
    asked = jnp.broadcast_to(asked[None], (X_SIZE,) + asked.shape).reshape(PEERS, rows, width)
    asked = lax.all_to_all(asked, "ctx", 0, 0, tiled=True, axis_index_groups=XC_GROUPS)
    asked = hold(asked)
    asked = pltpu.with_memory_space_constraint(asked, pltpu.HBM)
    column = jnp.concatenate([turned[:, :width], turned[:, width:]], 0)
    column = jnp.broadcast_to(column[None], (X_SIZE,) + column.shape)
    column = lax.all_to_all(column, "ctx", 0, 0, tiled=True, axis_index_groups=X_GROUPS)
    column = turn(column)
    swap = [(i, i ^ 1) for i in range(blocks)]
    other = lax.ppermute(line, "ctx", swap)
    held = pltpu.with_memory_space_constraint(line, pltpu.HBM)
    weights = lax.all_gather(column, "ctx", axis=0, axis_index_groups=Y_GROUPS)
    weights = pltpu.with_memory_space_constraint(weights, pltpu.HBM)
    mirrored = lax.ppermute(weights, "ctx", swap)
    mirrored = pltpu.with_memory_space_constraint(mirrored, pltpu.HBM)

    def attend(own, *lines):
        count = CORES if own else PEERS
        out_shape = [jax.ShapeDtypeStruct((count, width + STAT_ROWS, rows), jnp.bfloat16)]
        out_specs = [pl.BlockSpec(memory_space=pltpu.VMEM)]
        if not own:
            out_shape.append(jax.ShapeDtypeStruct((SLOTS, rows, width), jnp.bfloat16))
            out_specs.append(pl.BlockSpec(memory_space=pltpu.HBM))
        return pl.pallas_call(
            functools.partial(attend_kernel, own, rows, heads),
            out_shape=out_shape,
            in_specs=[
                pl.BlockSpec(memory_space=pltpu.SMEM),
                pl.BlockSpec(memory_space=pltpu.HBM),
            ] + [pl.BlockSpec(memory_space=pl.ANY)] * len(lines),
            out_specs=out_specs,
            scratch_shapes=[
                pltpu.SMEM((SLOTS + 1,), jnp.int32),
                pltpu.VMEM((PEERS, rows, width), jnp.bfloat16),
                pltpu.VMEM((SLOTS, rows, width), jnp.bfloat16),
                pltpu.VMEM((8, heads * rows), jnp.float32),
                pltpu.VMEM((8, heads * rows), jnp.float32),
                pltpu.VMEM((HEAD_FEATURES, heads * rows), jnp.float32),
                pltpu.SemaphoreType.DMA((4,)),
            ],
            compiler_params=pltpu.CompilerParams(
                vmem_limit_bytes=(32 << 20) if own else 62900000),
            cost_estimate=pl.CostEstimate(
                flops=1_000_000_000 * count, transcendentals=1_000_000 * count,
                bytes_accessed=5_000_000),
        )(placement, asked, *lines)

    parts, kept = attend(False, held, other)
    kept = pltpu.with_memory_space_constraint(kept, pltpu.HBM)
    gathered = lax.all_to_all(parts, "ctx", 0, 0, tiled=True, axis_index_groups=XC_GROUPS)
    near, = attend(True, kept)
    mate = hold(lax.ppermute(near[1:], "ctx", swap))
    mate = pltpu.with_memory_space_constraint(mate, pltpu.HBM)

    out_columns = blocks * turned.shape[0] // groups
    terms = pl.pallas_call(
        functools.partial(merge_kernel, rows, heads, groups),
        out_shape=jax.ShapeDtypeStruct((groups, rows, out_columns), jnp.bfloat16),
        in_specs=[
            pl.BlockSpec(memory_space=pltpu.VMEM),
        ] + [pl.BlockSpec(memory_space=pl.ANY)] * 2 + [pl.BlockSpec(memory_space=pltpu.HBM)] * 4,
        out_specs=pl.BlockSpec(memory_space=pltpu.VMEM),
        scratch_shapes=[
            pltpu.VMEM((rows, columns), jnp.bfloat16),
            pltpu.VMEM((CORES, width + STAT_ROWS, rows), jnp.bfloat16),
            pltpu.VMEM((X_SIZE, CORES, Y_SIZE) + weights.shape[-2:], jnp.bfloat16),
            pltpu.SemaphoreType.DMA((PEERS,)),
            pltpu.SemaphoreType.DMA((2,)),
        ],
        compiler_params=pltpu.CompilerParams(vmem_limit_bytes=32 * 1024 * 1024),
        name="merge_project",
    )(gathered, near, mate, held, other, weights, mirrored)
    return lax.psum_scatter(
        terms.reshape(groups * rows, out_columns), "head", scatter_dimension=0, tiled=True
    )


def solution(mesh):
    placed = (P(), P("ctx", "head"), P("ctx", "head"), P("ctx", "head"), P("head", "ctx"))

    return jax.shard_map(
        body, mesh=mesh, in_specs=placed, out_specs=P("ctx", "head"), check_vma=False
    )
```
